128 devices in a mesh: scen: 32 (over x, z, core), rep: 4 (over y).
Axes of the slice: x: 4, y: 4, z: 4, core: 2. Of those that a mesh axis runs over, the one named last changes fastest.
Arguments:
- scenarios: bfloat16 [32768, 16384], P('scen', 'rep'), may hold values from -24 to 24, as said below
- rep_index: int32 [1024], replicated, may hold values from 0 to 32767, as said below
Outputs:
- scen_potential: float32 [32768], P('scen')
- rep_potential: float32 [1024], P('rep')
- membership: bfloat16 [1024, 32768], P('rep', 'scen')
The draws below stay inside these ranges and needn't reach their ends.
Inputs may be any that keep to these rules, and one draw needn't show every extreme that they name: `rep_index`: the entries are distinct scenario numbers; each aligned block of 1024 consecutive scenarios holds exactly 32 of them. `scenarios`: finite surge values.
All inputs are finite; a program needn't handle non-finite values.
Results may differ from the reference program's by a relative error of at most 0.0035.
Values may be sent and summed in bfloat16 or wider, within the bound.
A program may use at most 64 MiB of HBM per device.

```python
import math
import jax
import jax.numpy as jnp
from jax import lax

S_DEV = 1024
F = 16384
ITERS = 3
S = 32768
R = 1024


def draw_scenarios(key, part):
    key_base = jax.random.fold_in(key, 11)
    key_z, key_s = jax.random.split(key_base, 2)
    noise = jnp.clip(jax.random.normal(key_z, (S, F), jnp.float32), -6.0, 6.0)
    scales = jnp.exp(jax.random.uniform(key_s, (S, 1), jnp.float32, jnp.log(0.5), jnp.log(2.0)))
    values = scales * noise
    return values.astype(jnp.bfloat16)


def draw_rep_index(key, part):
    key_base = jax.random.fold_in(key, 23)
    key_pick, key_order = jax.random.split(key_base)
    blocks = S // S_DEV
    per_block = R // blocks
    scores = jax.random.randint(key_pick, (blocks, S_DEV), 0, 2 ** 18, jnp.int32) * S_DEV
    scores = scores + jnp.arange(S_DEV, dtype=jnp.int32)[None, :]
    scores = scores.at[0, 0].set(-1)
    scores = scores.at[blocks - 1, S_DEV - 1].set(-2)
    picks = jnp.argsort(scores, axis=1)[:, :per_block].astype(jnp.int32)
    picks = picks + (jnp.arange(blocks, dtype=jnp.int32) * S_DEV)[:, None]
    flat = picks.reshape(R)
    order = jax.random.permutation(key_order, R)
    return flat[order].astype(jnp.int32)


def setup_inputs(seed: int = 0) -> dict:
    splits = jax.random.split(jax.random.key(seed), 3)
    scenarios = draw_scenarios(jax.random.fold_in(splits[2], 71), 0)
    rep_index = draw_rep_index(jax.random.fold_in(splits[2], 71), 0)
    return dict(scenarios=scenarios, rep_index=rep_index)


eps_blur = 0.1


def log_sum(score, axis):
    peak = jnp.max(score, axis=axis, keepdims=True)
    total = jnp.sum(jnp.exp(score - peak), axis=axis)
    return jnp.squeeze(peak, axis) + jnp.log(total)


def reference(scenarios, rep_index):
    reps = jnp.take(scenarios, rep_index, axis=0)
    sq_scen = jnp.sum(jnp.square(scenarios.astype(jnp.float32)), axis=1)
    sq_rep = jnp.sum(jnp.square(reps.astype(jnp.float32)), axis=1)
    cross = lax.dot_general(reps, scenarios, (((1,), (1,)), ((), ())), preferred_element_type=jnp.float32)
    cost = (sq_rep[:, None] + sq_scen[None, :] - 2.0 * cross) / F
    count_s = scenarios.shape[0]
    count_r = reps.shape[0]
    rep_pot = jnp.zeros((count_r,), jnp.float32)
    scen_pot = jnp.zeros((count_s,), jnp.float32)
    for step in range(ITERS):
        scen_pot = -eps_blur * math.log(count_s) - eps_blur * log_sum((rep_pot[:, None] - cost) / eps_blur, 0)
        rep_pot = -eps_blur * math.log(count_r) - eps_blur * log_sum((scen_pot[None, :] - cost) / eps_blur, 1)
    member = (count_s * jnp.exp((scen_pot[None, :] + rep_pot[:, None] - cost) / eps_blur)).astype(jnp.bfloat16)
    return scen_pot, rep_pot, member
```

```python
import functools
import math

import jax
import jax.numpy as jnp
from jax import lax
from jax.experimental import pallas as pl
from jax.experimental.pallas import tpu as pltpu
from jax.sharding import PartitionSpec as P

F = 16384
ITERS = 3
COUNT_S = 32768
COUNT_R = 1024
EPS = 0.1
FY = 4096
ROWS = 1024
EXT = FY + 128
HALF = 2048
MESH = pl.DeviceIdType.MESH
BF = jnp.bfloat16
F32 = jnp.float32
NT = (((1,), (1,)), ((), ()))


def remote(src, dst, ssem, rsem, dev):
    return pltpu.make_async_remote_copy(
        src_ref=src, dst_ref=dst, send_sem=ssem, recv_sem=rsem, device_id=dev, device_id_type=MESH
    )


def place():
    scen = lax.axis_index("scen")
    y = lax.axis_index("rep")
    return scen // 8, (scen // 2) % 4, scen % 2, y


def dev(x, z, c, y):
    return ((x * 4 + z) * 2 + c, y)


def barrier(peers):
    sem = pltpu.get_barrier_semaphore()
    for p in peers:
        pl.semaphore_signal(sem, inc=1, device_id=p, device_id_type=MESH)
    pl.semaphore_wait(sem, len(peers))


def column(row):
    return jnp.transpose(jnp.broadcast_to(row, (128, 128)))


def split3(v):
    hi = v.astype(BF)
    rest = v - hi.astype(F32)
    mid = rest.astype(BF)
    low = (rest - mid.astype(F32)).astype(BF)
    return hi, mid, low


def cost_kernel(rep_ref, scen_hbm, cost_ref, prow_ref, scen_v, reps_v, part, rcv1, rcv2, sqs,
                hbm_sem, f_send, f_recv, s_send, s_recv, c_send, c_recv, r1_send, r1_recv,
                r2_send, r2_recv):
    x, z, c, y = place()
    pf = x * (1 - c) + z * c
    ps = z * (1 - c) + x * c

    def along_first(d):
        return dev((x + (1 - c) * d) % 4, (z + c * d) % 4, c, y)

    def along_second(d):
        return dev((x + c * d) % 4, (z + (1 - c) * d) % 4, c, y)

    f_up, f_dn = along_first(1), along_first(3)
    s_up, s_dn = along_second(1), along_second(3)
    partner = dev(x, z, 1 - c, y)
    ya = y + 1 - 2 * (y % 2)
    yb = 3 - y
    at_y = lambda q: dev(x, z, c, q)

    loads = []
    for k in range(4):
        cols = pl.ds(k * 1024, 1024)
        cp = pltpu.make_async_copy(scen_hbm.at[:, cols], scen_v.at[:, cols], hbm_sem.at[k])
        cp.start()
        loads.append(cp)

    barrier([f_up, f_dn, s_up, s_dn, partner, at_y(ya), at_y(yb)])

    rep_i = rep_ref[...]
    rep_f = rep_i.astype(F32)
    counts = []
    cols_f = [column(rep_f[:, 128 * k:128 * k + 128]) for k in range(8)]
    for g in range(8):
        row = rep_f[:, 128 * g:128 * g + 128]
        acc = jnp.zeros((128, 128), F32)
        for k in range(8):
            acc = acc + jnp.where(cols_f[k] < row, 1.0, 0.0)
        counts.append(jnp.sum(acc, axis=0, keepdims=True))
    rank = jnp.concatenate(counts, axis=1)
    rank_i = rank.astype(jnp.int32)
    blk_i = rep_i >> 10
    bx, bz, bc = blk_i >> 3, (blk_i >> 1) & 3, blk_i & 1
    slot = jnp.where(bc == 0, bz * 4 + bx, 16 + bx * 4 + bz)
    prow_ref[...] = 32 * slot + rank_i - 32 * blk_i

    mine = (lax.axis_index("scen")).astype(F32)
    jot = lax.broadcasted_iota(jnp.int32, (32, ROWS), 0).astype(F32)
    hit = (rank - 32.0 * mine) == jot
    pos = jnp.sum(jnp.where(hit, rep_f, 0.0), axis=1, keepdims=True) - 1024.0 * mine
    sel = jnp.where(
        lax.broadcasted_iota(jnp.int32, (32, ROWS), 1).astype(F32) == pos, 1.0, 0.0
    ).astype(BF)

    def blk(t, cc, q, lo=0, hi=EXT):
        return reps_v.at[t, cc, pl.ds(pl.multiple_of(q * 32, 32), 32), pl.ds(lo, hi - lo)]

    sends = []

    def go(src, dst, ssem, rsem, to):
        cp = remote(src, dst, ssem, rsem, to)
        cp.start()
        sends.append(cp)

    qm, qp, q2 = (pf + 3) % 4, (pf + 1) % 4, (pf + 2) % 4
    parts = ((0, HALF), (HALF, EXT))

    def first(i, q, h, to):
        b = blk(0, c, q, *parts[h])
        go(b, b, f_send.at[i], f_recv.at[i], to)

    def first_wait(i, q, h):
        b = blk(0, c, q, *parts[h])
        remote(b, b, f_send.at[i], f_recv.at[i], f_up).wait_recv()

    total = jnp.zeros((32, 1), F32)
    for k in range(4):
        loads[k].wait()
        cols = slice(k * 1024, (k + 1) * 1024)
        own = jnp.dot(sel, scen_v[:, cols], preferred_element_type=F32)
        reps_v[0, c, pl.ds(pl.multiple_of(pf * 32, 32), 32), cols] = own.astype(BF)
        total = total + jnp.sum(own * own, axis=1, keepdims=True)
        if k == 1:
            first(0, pf, 0, f_up)
            first(2, pf, 0, f_dn)
    hi, mid, low = split3(total)
    lane = lax.broadcasted_iota(jnp.int32, (32, 128), 1)
    ext = jnp.where(lane == 0, hi.astype(F32),
                    jnp.where(lane == 1, mid.astype(F32),
                              jnp.where(lane == 2, low.astype(F32), 0.0)))
    reps_v[0, c, pl.ds(pl.multiple_of(pf * 32, 32), 32), FY:EXT] = ext.astype(BF)
    first(1, pf, 1, f_up)
    first(3, pf, 1, f_dn)

    def to_partner(t, i, q):
        b = blk(t, c, q)
        go(b, b, c_send.at[t, i], c_recv.at[t, i], partner)

    qs = [pf, qm, qp, q2]
    back = [2, 3, 0, 1]

    def second_up(i):
        go(blk(0, c, qs[i]), blk(1, c, qs[i]), s_send.at[0, i], s_recv.at[0, i], s_up)

    def second_dn(i):
        go(blk(0, c, qs[i]), blk(2, c, qs[i]), s_send.at[1, i], s_recv.at[1, i], s_dn)

    to_partner(0, 0, pf)

    def norms(i, _):
        rows = pl.ds(pl.multiple_of(i * 128, 128), 128)
        acc = jnp.zeros((128, 128), F32)
        for k in range(32):
            v = scen_v[rows, k * 128:(k + 1) * 128].astype(F32)
            acc = acc + v * v
        sqs[rows, :] = jnp.broadcast_to(jnp.sum(acc, axis=1, keepdims=True), (128, 128))
        return 0

    lax.fori_loop(0, 8, norms, 0)

    first_wait(0, qm, 0)
    first(4, qm, 0, f_up)
    first_wait(3, qp, 1)
    first(5, qp, 1, f_dn)
    first_wait(1, qm, 1)
    to_partner(0, 1, qm)
    first_wait(2, qp, 0)
    to_partner(0, 2, qp)
    second_up(0)
    second_dn(2)
    second_up(1)
    first_wait(4, q2, 0)
    first_wait(5, q2, 1)
    to_partner(0, 3, q2)
    second_dn(3)
    second_up(2)
    second_dn(0)
    second_up(3)
    second_dn(1)

    pqs = [ps, (ps + 3) % 4, (ps + 1) % 4, (ps + 2) % 4]

    def partner_wait(t):
        for i in range(4):
            b = blk(t, 1 - c, pqs[i])
            remote(b, b, c_send.at[t, i], c_recv.at[t, i], partner).wait_recv()

    ones8 = jnp.ones((8, 128), BF)
    firsts, seconds = (ya, yb), (yb, ya)

    def matmul(t):
        ext = reps_v[t, :, :, FY:EXT].reshape(256, 128)
        sqr = lax.dot_general(ones8, ext, NT, preferred_element_type=F32)[0:1, :]

        def tile(m, _):
            rows = pl.ds(pl.multiple_of(m * 256, 256), 256)
            cross = lax.dot_general(
                scen_v[rows, :], reps_v[t, :, :, 0:FY].reshape(256, FY), NT,
                preferred_element_type=F32)
            sq = sqs[rows, :]
            part[t, 0, m] = (sq + sqr[:, :128]) - 2.0 * cross[:, :128]
            part[t, 1, m] = (sq + sqr[:, 128:]) - 2.0 * cross[:, 128:]
            return 0

        lax.fori_loop(0, 4, tile, 0)
        for h in range(2):
            one = firsts[h]
            other = (3 - one) if h == 0 else (one + 1 - 2 * (one % 2))
            for k, d in ((1, other), (0, one)):
                go(part.at[t, h, d], rcv1.at[t, h, k], r1_send.at[t, h, k], r1_recv.at[t, h, k],
                   at_y(one))

    def reduce2(t):
        for h in range(2):
            d = seconds[h]
            buf = rcv1.at[t, h, 1]
            remote(buf, buf, r1_send.at[t, h, 1], r1_recv.at[t, h, 1], at_y(firsts[h])).wait_recv()
            part[t, h, d] = part[t, h, d] + rcv1[t, h, 1]
            go(part.at[t, h, d], rcv2.at[t, h], r2_send.at[t, h], r2_recv.at[t, h], at_y(d))

    shift = (0, 3, 1, 2)

    def finish(t):
        for h in range(2):
            buf = rcv1.at[t, h, 0]
            remote(buf, buf, r1_send.at[t, h, 0], r1_recv.at[t, h, 0], at_y(firsts[h])).wait_recv()
            buf = rcv2.at[t, h]
            remote(buf, buf, r2_send.at[t, h], r2_recv.at[t, h], at_y(seconds[h])).wait_recv()
            g = (z + shift[t]) % 4 if h == 0 else 4 + (x + shift[t]) % 4
            whole = part[t, h, y] + rcv1[t, h, 0] + rcv2[t, h]
            cost_ref[g] = whole * (1.0 / (F * EPS))

    def arrive_up(i):
        b = blk(1, c, qs[i])
        remote(b, b, s_send.at[0, i], s_recv.at[0, i], s_up).wait_recv()
        if i < 2:
            go(b, blk(3, c, qs[i]), s_send.at[2, i], s_recv.at[2, i], s_up)
        to_partner(1, i, qs[i])

    def arrive_dn(i):
        b = blk(2, c, qs[i])
        remote(b, b, s_send.at[1, i], s_recv.at[1, i], s_dn).wait_recv()
        if i >= 2:
            go(b, blk(3, c, qs[i]), s_send.at[2, i], s_recv.at[2, i], s_dn)
        to_partner(2, i, qs[i])

    def arrive_far(i):
        b = blk(3, c, qs[i])
        remote(b, b, s_send.at[2, i], s_recv.at[2, i], s_up).wait_recv()
        to_partner(3, i, qs[i])

    partner_wait(0)
    matmul(0)
    for i in range(2):
        arrive_up(i)
        arrive_dn(back[i])
    reduce2(0)
    for i in range(2, 4):
        arrive_up(i)
        arrive_dn(back[i])
    partner_wait(1)
    matmul(1)
    partner_wait(2)
    matmul(2)
    for i in (0, 2, 1, 3):
        arrive_far(i)
    reduce2(1)
    partner_wait(3)
    matmul(3)
    reduce2(2)
    finish(0)
    finish(1)
    reduce2(3)
    finish(2)
    finish(3)
    for cp in sends:
        cp.wait_send()


def sink_kernel(cost_ref, prow_ref, u_ref, v_ref, mem_ref, pi, u_buf, in1, in2, box1, box2, m_buf,
                s1, r1, s2, r2, su, ru, sm, rm):
    x, z, c, y = place()
    plane = x * 4 + z
    near = []
    for k in range(1, 8):
        q = (y * 2 + c + k) % 8
        near.append(dev(x, z, q % 2, q // 2))
    far = []
    for k in range(1, 16):
        q = (plane + k) % 16
        far.append(dev(q // 4, q % 4, c, y))
    ring = [dev(x, z, c, (y + k) % 4) for k in range(1, 4)]
    me1 = y * 2 + c
    barrier(near + far)
    sends = []

    def go(src, dst, ssem, rsem, to):
        cp = remote(src, dst, ssem, rsem, to)
        cp.start()
        sends.append(cp)

    def permutation():
        prow = prow_ref[...].astype(F32)
        for k in range(8):
            col = column(prow[:, 128 * k:128 * k + 128])
            for g in range(8):
                lane = lax.broadcasted_iota(jnp.int32, (128, 128), 1).astype(F32) + 128.0 * g
                pi[128 * k:128 * k + 128, 128 * g:128 * g + 128] = jnp.where(
                    col == lane, 1.0, 0.0).astype(BF)

    def lse(rows):
        peak = functools.reduce(jnp.maximum, rows)
        return peak + jnp.log(functools.reduce(jnp.add, [jnp.exp(r - peak) for r in rows]))

    v = jnp.zeros((8, 128), F32)
    u = None
    for it in range(ITERS):
        peak = None
        for g in range(8):
            s = v[g:g + 1, :] - cost_ref[g]
            peak = s if peak is None else jnp.maximum(peak, s)
        peak = jnp.max(peak, axis=1, keepdims=True)
        acc = None
        for g in range(8):
            e = jnp.exp((v[g:g + 1, :] - cost_ref[g]) - peak)
            acc = e if acc is None else acc + e
        u = -math.log(COUNT_S) - (peak + jnp.log(jnp.sum(acc, axis=1, keepdims=True)))
        rows = []
        for g in range(8):
            s = u - cost_ref[g]
            top = jnp.max(s, axis=0, keepdims=True)
            rows.append(top + jnp.log(jnp.sum(jnp.exp(s - top), axis=0, keepdims=True)))
        box1[it] = jnp.concatenate(rows, axis=0)
        for k in range(7):
            go(box1.at[it], in1.at[it, me1], s1.at[it, k], r1.at[it, k], near[k])
        in1[it, me1] = box1[it]
        if it == 0:
            permutation()
        if it == ITERS - 1:
            wide = jnp.broadcast_to(u, (256, 128))
            flat = [jnp.transpose(wide[128 * k:128 * k + 128, :])[0:1, :] for k in range(2)]
            u_buf[4] = jnp.concatenate(flat + [jnp.zeros((6, 128), F32)], axis=0) * EPS
            u_buf[y] = u_buf[4]
            for k in range(3):
                go(u_buf.at[4], u_buf.at[y], su.at[k], ru.at[k], ring[k])
        for k in range(7):
            q = (me1 + 7 - k) % 8
            b = in1.at[it, q]
            remote(b, b, s1.at[it, k], r1.at[it, k], near[k]).wait_recv()
        box2[it] = lse([in1[it, k] for k in range(8)])
        for k in range(15):
            go(box2.at[it], in2.at[it, plane], s2.at[it, k], r2.at[it, k], far[k])
        in2[it, plane] = box2[it]
        for k in range(15):
            q = (plane + 15 - k) % 16
            b = in2.at[it, q]
            remote(b, b, s2.at[it, k], r2.at[it, k], far[k]).wait_recv()
        v = -math.log(COUNT_R) - lse([in2[it, k] for k in range(16)])

    plan = []
    for g in range(8):
        plan.append((COUNT_S * jnp.exp((u + v[g:g + 1, :]) - cost_ref[g])).astype(BF))
    plan = jnp.concatenate(plan, axis=1)

    def rows_of(q):
        return pi[pl.ds(pl.multiple_of(q * 256, 256), 256), :]

    here = pl.ds(pl.multiple_of(y * 256, 256), 256)
    for n, k in enumerate((1, 0, 2)):
        q = (y + 1 + k) % 4
        m_buf[k] = lax.dot_general(rows_of(q), plan, NT, preferred_element_type=F32).astype(BF)
        go(m_buf.at[k], mem_ref.at[:, here], sm.at[k], rm.at[k], ring[k])
    mem_ref[:, here] = lax.dot_general(
        rows_of(y), plan, NT, preferred_element_type=F32).astype(BF)
    flat = jnp.concatenate([v[g:g + 1, :] for g in range(8)], axis=1)
    pieces = split3(flat)
    row = lax.broadcasted_iota(jnp.int32, (8, 1024), 0)
    three = jnp.where(row == 0, pieces[0].astype(F32),
                      jnp.where(row == 1, pieces[1].astype(F32),
                                jnp.where(row == 2, pieces[2].astype(F32), 0.0))).astype(BF)
    got = lax.dot_general(three, rows_of(y), NT, preferred_element_type=F32)
    v_ref[...] = (got[0:1, :] + got[1:2, :] + got[2:3, :]) * EPS
    for k in range(3):
        q = (y + 3 - k) % 4
        b = u_buf.at[q]
        remote(b, b, su.at[k], ru.at[k], ring[k]).wait_recv()
    u_ref[...] = jnp.concatenate([u_buf[k, 0:2, :] for k in range(4)], axis=0)
    for k in range(3):
        q = (y + 3 - k) % 4
        b = mem_ref.at[:, pl.ds(pl.multiple_of(q * 256, 256), 256)]
        remote(b, b, sm.at[k], rm.at[k], ring[k]).wait_recv()
    for cp in sends:
        cp.wait_send()


VM = pl.BlockSpec(memory_space=pltpu.VMEM)


def on_device(scenarios, rep_index):
    dma = pltpu.SemaphoreType.DMA
    cost, prow = pl.pallas_call(
        cost_kernel,
        out_shape=(jax.ShapeDtypeStruct((8, 256, 128), F32),
                   jax.ShapeDtypeStruct((1, 1024), jnp.int32)),
        in_specs=[VM, pl.BlockSpec(memory_space=pl.ANY)],
        out_specs=(VM, VM),
        scratch_shapes=[
            pltpu.VMEM((ROWS, FY), BF),
            pltpu.VMEM((4, 2, 128, EXT), BF),
            pltpu.VMEM((4, 2, 4, 256, 128), F32),
            pltpu.VMEM((4, 2, 2, 256, 128), F32),
            pltpu.VMEM((4, 2, 256, 128), F32),
            pltpu.VMEM((ROWS, 128), F32),
            dma((4,)), dma((6,)), dma((6,)), dma((3, 4)), dma((3, 4)), dma((4, 4)), dma((4, 4)),
            dma((4, 2, 2)), dma((4, 2, 2)), dma((4, 2)), dma((4, 2)),
        ],
        compiler_params=pltpu.CompilerParams(
            collective_id=0, has_side_effects=True, vmem_limit_bytes=48 << 20),
        name="cost",
    )(rep_index.reshape(1, 1024), scenarios)
    u, v, member = pl.pallas_call(
        sink_kernel,
        out_shape=(jax.ShapeDtypeStruct((8, 128), F32),
                   jax.ShapeDtypeStruct((1, 256), F32),
                   jax.ShapeDtypeStruct((256, 1024), BF)),
        in_specs=[VM, VM],
        out_specs=(VM, VM, VM),
        scratch_shapes=[
            pltpu.VMEM((1024, 1024), BF),
            pltpu.VMEM((5, 8, 128), F32),
            pltpu.VMEM((3, 8, 8, 128), F32),
            pltpu.VMEM((3, 16, 8, 128), F32),
            pltpu.VMEM((3, 8, 128), F32),
            pltpu.VMEM((3, 8, 128), F32),
            pltpu.VMEM((3, 256, 256), BF),
            dma((3, 7)), dma((3, 7)), dma((3, 15)), dma((3, 15)), dma((3,)), dma((3,)),
            dma((3,)), dma((3,)),
        ],
        compiler_params=pltpu.CompilerParams(
            collective_id=1, has_side_effects=True, vmem_limit_bytes=32 << 20),
        name="sinkhorn",
    )(cost, prow)
    return u.reshape(1024), v.reshape(256), member


def solution(mesh):
    return jax.shard_map(
        on_device,
        mesh=mesh,
        in_specs=(P("scen", "rep"), P()),
        out_specs=(P("scen"), P("rep"), P("rep", "scen")),
        check_vma=False,
    )
```

```python
import functools
import math

import jax
import jax.numpy as jnp
from jax import lax
from jax.experimental import pallas as pl
from jax.experimental.pallas import tpu as pltpu
from jax.sharding import PartitionSpec as P

F = 16384
ITERS = 3
COUNT_S = 32768
COUNT_R = 1024
EPS = 0.1
FY = 4096
ROWS = 1024
EXT = FY + 128
HALF = 2048
MESH = pl.DeviceIdType.MESH
BF = jnp.bfloat16
F32 = jnp.float32
NT = (((1,), (1,)), ((), ()))


def remote(src, dst, ssem, rsem, dev):
    return pltpu.make_async_remote_copy(
        src_ref=src, dst_ref=dst, send_sem=ssem, recv_sem=rsem, device_id=dev, device_id_type=MESH
    )


def place():
    scen = lax.axis_index("scen")
    y = lax.axis_index("rep")
    return scen // 8, (scen // 2) % 4, scen % 2, y


def dev(x, z, c, y):
    return ((x * 4 + z) * 2 + c, y)


def greet(peers):
    sem = pltpu.get_barrier_semaphore()
    for p in peers:
        pl.semaphore_signal(sem, inc=1, device_id=p, device_id_type=MESH)


def meet(count):
    pl.semaphore_wait(pltpu.get_barrier_semaphore(), count)


def column(row):
    return jnp.transpose(jnp.broadcast_to(row, (128, 128)))


def split3(v):
    hi = v.astype(BF)
    rest = v - hi.astype(F32)
    mid = rest.astype(BF)
    low = (rest - mid.astype(F32)).astype(BF)
    return hi, mid, low


def pack(x, scale):
    q = [jnp.round(x[64 * k:64 * k + 64] * scale).astype(jnp.int32) for k in range(4)]
    return jnp.concatenate(
        [(q[k] << 8) | ((q[3] >> (8 * k)) & 255) for k in range(3)], axis=0)


def unpack(w, scale):
    w = [w[64 * k:64 * k + 64] for k in range(3)]
    last = ((w[2] << 24) >> 8) | ((w[1] & 255) << 8) | (w[0] & 255)
    q = [w[0] >> 8, w[1] >> 8, w[2] >> 8, last]
    return jnp.concatenate(q, axis=0).astype(F32) * (1.0 / scale)


SCALE1 = 3.5
SCALE2 = 1.75


def lse(rows):
    peak = functools.reduce(jnp.maximum, rows)
    return peak + jnp.log(functools.reduce(jnp.add, [jnp.exp(r - peak) for r in rows]))


def kernel(rep_hbm, scen_hbm, u_ref, v_ref, mem_ref,
           scen_v, reps_v, part, snd1, rcv1, snd2, rcv2, sqs, cost, rep_v, pi, sq_buf,
           u_buf, in1, in2, box1, box2, split, row_snd, row_cost, relay,
           hbm_sem, f_send, f_recv, s_send, s_recv, c_send, c_recv, r1_send, r1_recv,
           r2_send, r2_recv, q_send, q_recv, s1, r1, s2, r2, su, ru, sm, rm):
    x, z, c, y = place()
    pf = x * (1 - c) + z * c
    ps = z * (1 - c) + x * c

    def along_first(d):
        return dev((x + (1 - c) * d) % 4, (z + c * d) % 4, c, y)

    def along_second(d):
        return dev((x + c * d) % 4, (z + (1 - c) * d) % 4, c, y)

    f_up, f_dn = along_first(1), along_first(3)
    s_up, s_dn = along_second(1), along_second(3)
    partner = dev(x, z, 1 - c, y)
    ya = y + 1 - 2 * (y % 2)
    yb = 3 - y
    yc = (y + 2) % 4
    at_y = lambda q: dev(x, z, c, q)
    plane = x * 4 + z
    me1 = y * 2 + c
    near, far = [], []
    for k in range(1, 8):
        q = (me1 + k) % 8
        near.append(dev(x, z, q % 2, q // 2))
    for k in range(1, 16):
        q = (plane + k) % 16
        far.append(dev(q // 4, q % 4, c, y))
    ring = [at_y((y + k) % 4) for k in range(1, 4)]

    rep_load = pltpu.make_async_copy(rep_hbm, rep_v, hbm_sem.at[4])
    rep_load.start()
    loads = []
    for k in range(4):
        cols = pl.ds(k * 1024, 1024)
        cp = pltpu.make_async_copy(scen_hbm.at[:, cols], scen_v.at[:, cols], hbm_sem.at[k])
        cp.start()
        loads.append(cp)
    greet(near + far)
    rep_load.wait()

    rep_i = rep_v[...]
    rep_f = rep_i.astype(F32)
    counts = []
    cols_f = [column(rep_f[:, 128 * k:128 * k + 128]) for k in range(8)]
    for g in range(8):
        row = rep_f[:, 128 * g:128 * g + 128]
        acc = jnp.zeros((128, 128), F32)
        for k in range(8):
            acc = acc + jnp.where(cols_f[k] < row, 1.0, 0.0)
        counts.append(jnp.sum(acc, axis=0, keepdims=True))
    rank = jnp.concatenate(counts, axis=1)
    rank_i = rank.astype(jnp.int32)
    blk_i = rep_i >> 10
    bx, bz, bc = blk_i >> 3, (blk_i >> 1) & 3, blk_i & 1
    slot = jnp.where(bc == 0, bz * 4 + bx, 16 + bx * 4 + bz)
    prow = (32 * slot + rank_i - 32 * blk_i).astype(F32)

    mine = (lax.axis_index("scen")).astype(F32)
    jot = lax.broadcasted_iota(jnp.int32, (32, ROWS), 0).astype(F32)
    hit = (rank - 32.0 * mine) == jot
    pos = jnp.sum(jnp.where(hit, rep_f, 0.0), axis=1, keepdims=True) - 1024.0 * mine
    sel = jnp.where(
        lax.broadcasted_iota(jnp.int32, (32, ROWS), 1).astype(F32) == pos, 1.0, 0.0
    ).astype(BF)

    def blk(t, cc, q, lo=0, hi=EXT):
        return reps_v.at[t, cc, pl.ds(pl.multiple_of(q * 32, 32), 32), pl.ds(lo, hi - lo)]

    sends = []

    def go(src, dst, ssem, rsem, to):
        cp = remote(src, dst, ssem, rsem, to)
        cp.start()
        sends.append(cp)

    def recv(buf, ssem, rsem):
        remote(buf, buf, ssem, rsem, partner).wait_recv()

    qm, qp, q2 = (pf + 3) % 4, (pf + 1) % 4, (pf + 2) % 4
    parts = ((0, HALF), (HALF, EXT))

    def first(i, q, h, to):
        b = blk(0, c, q, *parts[h])
        go(b, b, f_send.at[i], f_recv.at[i], to)

    def first_wait(i, q, h):
        recv(blk(0, c, q, *parts[h]), f_send.at[i], f_recv.at[i])

    total = jnp.zeros((32, 1), F32)
    for k in range(4):
        loads[k].wait()
        cols = slice(k * 1024, (k + 1) * 1024)
        own = jnp.dot(sel, scen_v[:, cols], preferred_element_type=F32)
        reps_v[0, c, pl.ds(pl.multiple_of(pf * 32, 32), 32), cols] = own.astype(BF)
        total = total + jnp.sum(own * own, axis=1, keepdims=True)
        if k == 1:
            meet(22)
            first(0, pf, 0, f_up)
            first(2, pf, 0, f_dn)
    hi, mid, low = split3(total)
    lane = lax.broadcasted_iota(jnp.int32, (32, 128), 1)
    ext = jnp.where(lane == 0, hi.astype(F32),
                    jnp.where(lane == 1, mid.astype(F32),
                              jnp.where(lane == 2, low.astype(F32), 0.0)))
    reps_v[0, c, pl.ds(pl.multiple_of(pf * 32, 32), 32), FY:EXT] = ext.astype(BF)
    first(1, pf, 1, f_up)
    first(3, pf, 1, f_dn)

    def to_partner(t, i, q):
        b = blk(t, c, q)
        go(b, b, c_send.at[t, i], c_recv.at[t, i], partner)

    qs = [pf, qm, qp, q2]
    back = [2, 3, 0, 1]

    def second_up(i):
        go(blk(0, c, qs[i]), blk(1, c, qs[i]), s_send.at[0, i], s_recv.at[0, i], s_up)

    def second_dn(i):
        go(blk(0, c, qs[i]), blk(2, c, qs[i]), s_send.at[1, i], s_recv.at[1, i], s_dn)

    to_partner(0, 0, pf)

    def norms(i, _):
        rows = pl.ds(pl.multiple_of(i * 128, 128), 128)
        acc = jnp.zeros((128, 128), F32)
        for k in range(32):
            v = scen_v[rows, k * 128:(k + 1) * 128].astype(F32)
            acc = acc + v * v
        wide = jnp.broadcast_to(jnp.sum(acc, axis=1, keepdims=True), (128, 128))
        sqs[i] = jnp.transpose(wide)[0:8, :]
        return 0

    lax.fori_loop(0, 8, norms, 0)

    def permutation():
        for k in range(8):
            col = column(prow[:, 128 * k:128 * k + 128])
            for g in range(8):
                lane = lax.broadcasted_iota(jnp.int32, (128, 128), 1).astype(F32) + 128.0 * g
                pi[128 * k:128 * k + 128, 128 * g:128 * g + 128] = jnp.where(
                    col == lane, 1.0, 0.0).astype(BF)

    first_wait(0, qm, 0)
    first(4, qm, 0, f_up)
    first_wait(3, qp, 1)
    first(5, qp, 1, f_dn)
    first_wait(1, qm, 1)
    to_partner(0, 1, qm)
    first_wait(2, qp, 0)
    to_partner(0, 2, qp)
    second_up(0)
    second_dn(2)
    second_up(1)
    permutation()
    first_wait(4, q2, 0)
    first_wait(5, q2, 1)
    to_partner(0, 3, q2)
    second_dn(3)
    second_up(2)
    second_dn(0)
    second_up(3)
    second_dn(1)

    pqs = [ps, (ps + 3) % 4, (ps + 1) % 4, (ps + 2) % 4]

    def partner_wait(t):
        for i in range(4):
            recv(blk(t, 1 - c, pqs[i]), c_send.at[t, i], c_recv.at[t, i])

    ones8 = jnp.ones((8, 128), BF)
    firsts, seconds = (ya, yb), (yb, ya)
    shift = (0, 3, 1, 2)
    groups = [((z + d) % 4, 4 + (x + d) % 4) for d in shift]

    def send1(t, h, k):
        return remote(snd1.at[t, h, k], rcv1.at[t, h, k], r1_send.at[t, h, k], r1_recv.at[t, h, k],
                      at_y(firsts[h]))

    def matmul(t):
        ext = reps_v[t, :, :, FY:EXT].reshape(256, 128)
        sqr = lax.dot_general(ones8, ext, NT, preferred_element_type=F32)
        for h in range(2):
            sq_buf[y, groups[t][h]] = sqr[:, 128 * h:128 * h + 128]

        def tile(m, _):
            d = jnp.where(m == 0, yc, jnp.where(m == 1, ya, jnp.where(m == 2, yb, y)))
            cross = lax.dot_general(
                scen_v[pl.ds(pl.multiple_of(d * 256, 256), 256), :],
                reps_v[t, :, :, 0:FY].reshape(256, FY), NT, preferred_element_type=F32)
            lo, hi = cross[:, :128], cross[:, 128:]
            part[t, 0, m] = lo
            part[t, 1, m] = hi

            @pl.when(m == 0)
            def _():
                snd1[t, 0, 1] = pack(lo, SCALE1)
                send1(t, 0, 1).start()
                snd1[t, 1, 1] = pack(hi, SCALE1)
                send1(t, 1, 1).start()

            @pl.when(m == 1)
            def _():
                snd1[t, 0, 0] = pack(lo, SCALE1)
                send1(t, 0, 0).start()

            @pl.when(m == 2)
            def _():
                snd1[t, 1, 0] = pack(hi, SCALE1)
                send1(t, 1, 0).start()

            return 0

        lax.fori_loop(0, 4, tile, 0)
        for h in range(2):
            for k in range(2):
                sends.append(send1(t, h, k))

    def reduce2(t):
        for h in range(2):
            recv(rcv1.at[t, h, 1], r1_send.at[t, h, 1], r1_recv.at[t, h, 1])
            snd2[t, h] = pack(part[t, h, 2 - h] + unpack(rcv1[t, h, 1], SCALE1), SCALE2)
            go(snd2.at[t, h], rcv2.at[t, h], r2_send.at[t, h], r2_recv.at[t, h], at_y(seconds[h]))

    def finish(t):
        for h in range(2):
            recv(rcv1.at[t, h, 0], r1_send.at[t, h, 0], r1_recv.at[t, h, 0])
            recv(rcv2.at[t, h], r2_send.at[t, h], r2_recv.at[t, h])
            whole = part[t, h, 3] + unpack(rcv1[t, h, 0], SCALE1) + unpack(rcv2[t, h], SCALE2)
            g = groups[t][h]
            sq_r = sq_buf[0, g] + sq_buf[1, g] + sq_buf[2, g] + sq_buf[3, g]
            cost[g] = ((sq_s + sq_r[0:1, :]) - 2.0 * whole) * (1.0 / (F * EPS))

    def arrive_up(i):
        b = blk(1, c, qs[i])
        recv(b, s_send.at[0, i], s_recv.at[0, i])
        if i < 2:
            go(b, blk(3, c, qs[i]), s_send.at[2, i], s_recv.at[2, i], s_up)
        to_partner(1, i, qs[i])

    def arrive_dn(i):
        b = blk(2, c, qs[i])
        recv(b, s_send.at[1, i], s_recv.at[1, i])
        if i >= 2:
            go(b, blk(3, c, qs[i]), s_send.at[2, i], s_recv.at[2, i], s_dn)
        to_partner(2, i, qs[i])

    def arrive_far(i):
        recv(blk(3, c, qs[i]), s_send.at[2, i], s_recv.at[2, i])
        to_partner(3, i, qs[i])

    partner_wait(0)
    matmul(0)
    for i in range(2):
        arrive_up(i)
        arrive_dn(back[i])
    reduce2(0)
    for i in range(2, 4):
        arrive_up(i)
        arrive_dn(back[i])
    partner_wait(1)
    matmul(1)
    arrive_far(0)
    arrive_far(2)
    partner_wait(2)
    matmul(2)
    arrive_far(1)
    arrive_far(3)
    reduce2(1)
    partner_wait(3)
    matmul(3)
    sq_buf[y, 8] = jnp.concatenate([sqs[k, 0:1, :] for k in range(8)], axis=0)
    for k in range(3):
        go(sq_buf.at[y], sq_buf.at[y], q_send.at[k], q_recv.at[k], ring[k])
    reduce2(2)
    for k in range(3):
        recv(sq_buf.at[(y + 3 - k) % 4], q_send.at[k], q_recv.at[k])
    sq_all = sq_buf[0, 8] + sq_buf[1, 8] + sq_buf[2, 8] + sq_buf[3, 8]
    sqs[0] = sq_all
    sq_s = jnp.concatenate(
        [column(sqs[0, pl.ds(2 * y + k, 1), :]) for k in range(2)], axis=0)
    finish(0)
    finish(1)
    reduce2(3)
    finish(2)
    finish(3)

    def rows_of(q):
        return pi[pl.ds(pl.multiple_of(q * 256, 256), 256), :]

    here = pl.ds(pl.multiple_of(y * 256, 256), 256)

    def permuted(q):
        out = None
        for k in range(3):
            some = lax.dot_general(rows_of(q), split[k], NT, preferred_element_type=F32)
            out = some if out is None else out + some
        return out

    def make_split():
        for g in range(8):
            for k, piece in enumerate(split3(cost[g])):
                split[k, :, 128 * g:128 * g + 128] = piece

    up, dn = ring[0], ring[2]

    v = jnp.zeros((8, 128), F32)
    for it in range(ITERS):
        peak = None
        for g in range(8):
            s = v[g:g + 1, :] - cost[g]
            peak = s if peak is None else jnp.maximum(peak, s)
        peak = jnp.max(peak, axis=1, keepdims=True)
        acc = None
        for g in range(8):
            e = jnp.exp((v[g:g + 1, :] - cost[g]) - peak)
            acc = e if acc is None else acc + e
        u = -math.log(COUNT_S) - (peak + jnp.log(jnp.sum(acc, axis=1, keepdims=True)))
        rows = []
        for g in range(8):
            s = u - cost[g]
            top = jnp.max(s, axis=0, keepdims=True)
            rows.append(top + jnp.log(jnp.sum(jnp.exp(s - top), axis=0, keepdims=True)))
        box1[it] = jnp.concatenate(rows, axis=0)
        for k in range(7):
            go(box1.at[it], in1.at[it, me1], s1.at[it, k], r1.at[it, k], near[k])
        in1[it, me1] = box1[it]
        if it == 0:
            make_split()
            row_snd[0] = permuted((y + 1) % 4)
            go(row_snd.at[0], row_cost.at[:, here], sm.at[0], rm.at[0], up)
            row_snd[1] = permuted((y + 3) % 4)
            go(row_snd.at[1], row_cost.at[:, here], sm.at[1], rm.at[1], dn)
        if it == 1:
            go(row_snd.at[2, 0:128], relay.at[0], sm.at[2], rm.at[2], up)
            go(row_snd.at[2, 128:256], relay.at[1], sm.at[3], rm.at[3], dn)
        if it == ITERS - 1:
            wide = jnp.broadcast_to(u, (256, 128))
            flat = [jnp.transpose(wide[128 * k:128 * k + 128, :])[0:1, :] for k in range(2)]
            u_buf[4] = jnp.concatenate(flat + [jnp.zeros((6, 128), F32)], axis=0)
            u_buf[y] = u_buf[4]
            for k in range(3):
                go(u_buf.at[4], u_buf.at[y], su.at[k], ru.at[k], ring[k])
        for k in range(7):
            recv(in1.at[it, (me1 + 7 - k) % 8], s1.at[it, k], r1.at[it, k])
        box2[it] = lse([in1[it, k] for k in range(8)])
        for k in range(15):
            go(box2.at[it], in2.at[it, plane], s2.at[it, k], r2.at[it, k], far[k])
        in2[it, plane] = box2[it]
        if it == 0:
            row_snd[2] = permuted(yc)
            row_cost[:, here] = permuted(y)
        if it == 1:
            recv(relay.at[0], sm.at[2], rm.at[2])
            there = pl.ds(pl.multiple_of(((y + 3) % 4) * 256, 256), 256)
            go(relay.at[0], row_cost.at[0:128, there], sm.at[4], rm.at[4], up)
            recv(relay.at[1], sm.at[3], rm.at[3])
            there = pl.ds(pl.multiple_of(((y + 1) % 4) * 256, 256), 256)
            go(relay.at[1], row_cost.at[128:256, there], sm.at[5], rm.at[5], dn)
        for k in range(15):
            recv(in2.at[it, (plane + 15 - k) % 16], s2.at[it, k], r2.at[it, k])
        v = -math.log(COUNT_R) - lse([in2[it, k] for k in range(16)])

    flat = jnp.concatenate([v[g:g + 1, :] for g in range(8)], axis=1)
    pieces = split3(flat)
    row = lax.broadcasted_iota(jnp.int32, (8, 1024), 0)
    three = jnp.where(row == 0, pieces[0].astype(F32),
                      jnp.where(row == 1, pieces[1].astype(F32),
                                jnp.where(row == 2, pieces[2].astype(F32), 0.0))).astype(BF)
    got = lax.dot_general(three, rows_of(y), NT, preferred_element_type=F32)
    v_row = got[0:1, :] + got[1:2, :] + got[2:3, :]
    v_ref[...] = v_row * EPS
    v_col = jnp.concatenate([column(v_row[:, 128 * k:128 * k + 128]) for k in range(2)], axis=0)
    for k in range(3):
        recv(u_buf.at[(y + 3 - k) % 4], su.at[k], ru.at[k])
    recv(row_cost.at[:, pl.ds(pl.multiple_of(((y + 3) % 4) * 256, 256), 256)], sm.at[0], rm.at[0])
    recv(row_cost.at[:, pl.ds(pl.multiple_of(((y + 1) % 4) * 256, 256), 256)], sm.at[1], rm.at[1])
    there = pl.ds(pl.multiple_of(yc * 256, 256), 256)
    recv(row_cost.at[0:128, there], sm.at[4], rm.at[4])
    recv(row_cost.at[128:256, there], sm.at[5], rm.at[5])
    for k in range(8):
        cols = slice(128 * k, 128 * k + 128)
        u_row = u_buf[k // 2, k % 2:k % 2 + 1, :]
        mem_ref[:, cols] = (COUNT_S * jnp.exp((u_row + v_col) - row_cost[:, cols])).astype(BF)
    u_ref[...] = jnp.concatenate([u_buf[k, 0:2, :] for k in range(4)], axis=0) * EPS
    for cp in sends:
        cp.wait_send()


VM = pl.BlockSpec(memory_space=pltpu.VMEM)


def on_device(scenarios, rep_index):
    dma = pltpu.SemaphoreType.DMA
    u, v, member = pl.pallas_call(
        kernel,
        out_shape=(jax.ShapeDtypeStruct((8, 128), F32),
                   jax.ShapeDtypeStruct((1, 256), F32),
                   jax.ShapeDtypeStruct((256, 1024), BF)),
        in_specs=[pl.BlockSpec(memory_space=pl.ANY)] * 2,
        out_specs=(VM, VM, VM),
        scratch_shapes=[
            pltpu.VMEM((ROWS, FY), BF),
            pltpu.VMEM((4, 2, 128, EXT), BF),
            pltpu.VMEM((4, 2, 4, 256, 128), F32),
            pltpu.VMEM((4, 2, 2, 192, 128), jnp.int32),
            pltpu.VMEM((4, 2, 2, 192, 128), jnp.int32),
            pltpu.VMEM((4, 2, 192, 128), jnp.int32),
            pltpu.VMEM((4, 2, 192, 128), jnp.int32),
            pltpu.VMEM((8, 8, 128), F32),
            pltpu.VMEM((8, 256, 128), F32),
            pltpu.VMEM((1, 1024), jnp.int32),
            pltpu.VMEM((1024, 1024), BF),
            pltpu.VMEM((4, 9, 8, 128), F32),
            pltpu.VMEM((5, 8, 128), F32),
            pltpu.VMEM((3, 8, 8, 128), F32),
            pltpu.VMEM((3, 16, 8, 128), F32),
            pltpu.VMEM((3, 8, 128), F32),
            pltpu.VMEM((3, 8, 128), F32),
            pltpu.VMEM((3, 256, 1024), BF),
            pltpu.VMEM((3, 256, 256), F32),
            pltpu.VMEM((256, 1024), F32),
            pltpu.VMEM((2, 128, 256), F32),
            dma((5,)), dma((6,)), dma((6,)), dma((3, 4)), dma((3, 4)), dma((4, 4)), dma((4, 4)),
            dma((4, 2, 2)), dma((4, 2, 2)), dma((4, 2)), dma((4, 2)), dma((3,)), dma((3,)),
            dma((3, 7)), dma((3, 7)), dma((3, 15)), dma((3, 15)), dma((3,)), dma((3,)),
            dma((6,)), dma((6,)),
        ],
        compiler_params=pltpu.CompilerParams(
            collective_id=0, has_side_effects=True, vmem_limit_bytes=56 << 20),
        name="transport",
    )(rep_index.reshape(1, 1024), scenarios)
    return u.reshape(1024), v.reshape(256), member


def solution(mesh):
    return jax.shard_map(
        on_device,
        mesh=mesh,
        in_specs=(P("scen", "rep"), P()),
        out_specs=(P("scen"), P("rep"), P("rep", "scen")),
        check_vma=False,
    )
```

```python
import functools
import math

import jax
import jax.numpy as jnp
from jax import lax
from jax.experimental import pallas as pl
from jax.experimental.pallas import tpu as pltpu
from jax.sharding import PartitionSpec as P

F = 16384
ITERS = 3
COUNT_S = 32768
COUNT_R = 1024
EPS = 0.1
FY = 4096
ROWS = 1024
EXT = FY + 128
QUARTERS = ((0, 1024), (1024, 2048), (2048, 3072), (3072, EXT))
MESH = pl.DeviceIdType.MESH
BF = jnp.bfloat16
F32 = jnp.float32
NT = (((1,), (1,)), ((), ()))


def remote(src, dst, ssem, rsem, dev):
    return pltpu.make_async_remote_copy(
        src_ref=src, dst_ref=dst, send_sem=ssem, recv_sem=rsem, device_id=dev, device_id_type=MESH
    )


def place():
    scen = lax.axis_index("scen")
    y = lax.axis_index("rep")
    return scen // 8, (scen // 2) % 4, scen % 2, y


def dev(x, z, c, y):
    return ((x * 4 + z) * 2 + c, y)


def greet(peers):
    sem = pltpu.get_barrier_semaphore()
    for p in peers:
        pl.semaphore_signal(sem, inc=1, device_id=p, device_id_type=MESH)


def meet(count):
    pl.semaphore_wait(pltpu.get_barrier_semaphore(), count)


def column(row):
    return jnp.transpose(jnp.broadcast_to(row, (128, 128)))


def split3(v):
    hi = v.astype(BF)
    rest = v - hi.astype(F32)
    mid = rest.astype(BF)
    low = (rest - mid.astype(F32)).astype(BF)
    return hi, mid, low


def pack(x, scale):
    q = [jnp.round(x[64 * k:64 * k + 64] * scale).astype(jnp.int32) for k in range(4)]
    return jnp.concatenate(
        [(q[k] << 8) | ((q[3] >> (8 * k)) & 255) for k in range(3)], axis=0)


def unpack(w, scale):
    w = [w[64 * k:64 * k + 64] for k in range(3)]
    last = ((w[2] << 24) >> 8) | ((w[1] & 255) << 8) | (w[0] & 255)
    q = [w[0] >> 8, w[1] >> 8, w[2] >> 8, last]
    return jnp.concatenate(q, axis=0).astype(F32) * (1.0 / scale)


NEAR_ORDER = (3, 4, 2, 5, 1, 6, 0)
FAR_ORDER = tuple(sorted(range(15), key=lambda k: -(min((k + 1) % 4, 4 - (k + 1) % 4)
                                                   + min((k + 1) // 4, 4 - (k + 1) // 4))))
SCALE1 = 3.5
SCALE2 = 1.75


def lse(rows):
    peak = functools.reduce(jnp.maximum, rows)
    return peak + jnp.log(functools.reduce(jnp.add, [jnp.exp(r - peak) for r in rows]))


def kernel(rep_hbm, scen_hbm, u_ref, v_ref, row_cost,
           scen_v, reps_v, part, snd1, rcv1, snd2, rcv2, sqs, cost, rep_v, pi, sq_buf,
           u_buf, in1, in2, box1, box2, keep, split, row_snd, relay,
           hbm_sem, f_send, f_recv, s_send, s_recv, c_send, c_recv, r1_send, r1_recv,
           r2_send, r2_recv, q_send, q_recv, s1, r1, s2, r2, su, ru, sm, rm):
    x, z, c, y = place()
    pf = x * (1 - c) + z * c
    ps = z * (1 - c) + x * c

    def along_first(d):
        return dev((x + (1 - c) * d) % 4, (z + c * d) % 4, c, y)

    def along_second(d):
        return dev((x + c * d) % 4, (z + (1 - c) * d) % 4, c, y)

    f_up, f_dn = along_first(1), along_first(3)
    s_up, s_dn = along_second(1), along_second(3)
    partner = dev(x, z, 1 - c, y)
    ya = y + 1 - 2 * (y % 2)
    yb = 3 - y
    yc = (y + 2) % 4
    at_y = lambda q: dev(x, z, c, q)
    plane = x * 4 + z
    me1 = y * 2 + c
    near, far = [], []
    for k in range(1, 8):
        q = (me1 + k) % 8
        near.append(dev(x, z, q % 2, q // 2))
    for k in range(1, 16):
        q = (plane + k) % 16
        far.append(dev(q // 4, q % 4, c, y))
    ring = [at_y((y + k) % 4) for k in range(1, 4)]

    rep_load = pltpu.make_async_copy(rep_hbm, rep_v, hbm_sem.at[4])
    rep_load.start()
    loads = []
    for k in range(4):
        cols = pl.ds(k * 1024, 1024)
        cp = pltpu.make_async_copy(scen_hbm.at[:, cols], scen_v.at[:, cols], hbm_sem.at[k])
        cp.start()
        loads.append(cp)
    greet([f_up, f_dn, s_up, s_dn, partner, at_y(ya), at_y(yb)])
    rep_load.wait()

    rep_i = rep_v[...]
    rep_f = rep_i.astype(F32)
    counts = []
    cols_f = [column(rep_f[:, 128 * k:128 * k + 128]) for k in range(8)]
    for g in range(8):
        row = rep_f[:, 128 * g:128 * g + 128]
        acc = jnp.zeros((128, 128), F32)
        for k in range(8):
            acc = acc + jnp.where(cols_f[k] < row, 1.0, 0.0)
        counts.append(jnp.sum(acc, axis=0, keepdims=True))
    rank = jnp.concatenate(counts, axis=1)
    rank_i = rank.astype(jnp.int32)
    blk_i = rep_i >> 10
    bx, bz, bc = blk_i >> 3, (blk_i >> 1) & 3, blk_i & 1
    slot = jnp.where(bc == 0, bz * 4 + bx, 16 + bx * 4 + bz)
    prow = (32 * slot + rank_i - 32 * blk_i).astype(F32)

    mine = (lax.axis_index("scen")).astype(F32)
    jot = lax.broadcasted_iota(jnp.int32, (32, ROWS), 0).astype(F32)
    hit = (rank - 32.0 * mine) == jot
    pos = jnp.sum(jnp.where(hit, rep_f, 0.0), axis=1, keepdims=True) - 1024.0 * mine
    sel = jnp.where(
        lax.broadcasted_iota(jnp.int32, (32, ROWS), 1).astype(F32) == pos, 1.0, 0.0
    ).astype(BF)

    def blk(t, cc, r, lo=0, hi=EXT):
        return reps_v.at[t, cc, pl.ds(32 * r, 32), pl.ds(lo, hi - lo)]

    sends = []

    def go(src, dst, ssem, rsem, to):
        cp = remote(src, dst, ssem, rsem, to)
        cp.start()
        sends.append(cp)

    def flush():
        for cp in sends:
            cp.wait_send()
        sends.clear()

    def recv(buf, ssem, rsem):
        remote(buf, buf, ssem, rsem, partner).wait_recv()

    def first(i, r, to_r, h, to):
        go(blk(0, c, r, *QUARTERS[h]), blk(0, c, to_r, *QUARTERS[h]), f_send.at[i], f_recv.at[i], to)

    def first_wait(i, r, h):
        recv(blk(0, c, r, *QUARTERS[h]), f_send.at[i], f_recv.at[i])

    total = jnp.zeros((32, 1), F32)
    for k in range(4):
        loads[k].wait()
        cols = slice(k * 1024, (k + 1) * 1024)
        own = jnp.dot(sel, scen_v[:, cols], preferred_element_type=F32)
        reps_v[0, c, 0:32, cols] = own.astype(BF)
        total = total + jnp.sum(own * own, axis=1, keepdims=True)
        if k == 0:
            meet(7)
        if k < 3:
            first(k, 0, 3, k, f_up)
            first(4 + k, 0, 1, k, f_dn)
    hi, mid, low = split3(total)
    lane = lax.broadcasted_iota(jnp.int32, (32, 128), 1)
    ext = jnp.where(lane == 0, hi.astype(F32),
                    jnp.where(lane == 1, mid.astype(F32),
                              jnp.where(lane == 2, low.astype(F32), 0.0)))
    reps_v[0, c, 0:32, FY:EXT] = ext.astype(BF)
    first(3, 0, 3, 3, f_up)
    first(7, 0, 1, 3, f_dn)

    def to_partner(t, r):
        b = blk(t, c, r)
        go(b, b, c_send.at[t, r], c_recv.at[t, r], partner)

    def from_partner(t, r):
        recv(blk(t, 1 - c, r), c_send.at[t, r], c_recv.at[t, r])

    ahead, behind = (0, 3), (1, 2)

    def second_up(r):
        t = 1 if r in ahead else 2
        go(blk(0, c, r), blk(t, c, r), s_send.at[0, r], s_recv.at[0, r], s_up)

    def second_dn(r):
        t = 1 if r in behind else 2
        go(blk(0, c, r), blk(t, c, r), s_send.at[1, r], s_recv.at[1, r], s_dn)

    def arrive_up(r):
        t = 1 if r in ahead else 2
        b = blk(t, c, r)
        recv(b, s_send.at[0, r], s_recv.at[0, r])
        if t == 1:
            go(b, blk(3, c, r), s_send.at[2, r], s_recv.at[2, r], s_up)
        to_partner(t, r)

    def arrive_dn(r):
        t = 1 if r in behind else 2
        b = blk(t, c, r)
        recv(b, s_send.at[1, r], s_recv.at[1, r])
        if t == 1:
            go(b, blk(3, c, r), s_send.at[2, r], s_recv.at[2, r], s_dn)
        to_partner(t, r)

    def arrive_far(r):
        recv(blk(3, c, r), s_send.at[2, r], s_recv.at[2, r])
        to_partner(3, r)

    to_partner(0, 0)

    def norms(i, _):
        rows = pl.ds(pl.multiple_of(i * 128, 128), 128)
        acc = jnp.zeros((128, 128), F32)
        for k in range(32):
            v = scen_v[rows, k * 128:(k + 1) * 128].astype(F32)
            acc = acc + v * v
        wide = jnp.broadcast_to(jnp.sum(acc, axis=1, keepdims=True), (128, 128))
        sqs[i] = jnp.transpose(wide)[0:8, :]
        return 0

    def permutation():
        for k in range(8):
            col = column(prow[:, 128 * k:128 * k + 128])
            for g in range(8):
                lane = lax.broadcasted_iota(jnp.int32, (128, 128), 1).astype(F32) + 128.0 * g
                pi[128 * k:128 * k + 128, 128 * g:128 * g + 128] = jnp.where(
                    col == lane, 1.0, 0.0).astype(BF)

    for h in range(2):
        first_wait(h, 3, h)
        first(8 + h, 3, 2, h, f_up)
    second_up(0)
    first_wait(4, 1, 0)
    first_wait(5, 1, 1)
    for h in range(2, 4):
        first_wait(4 + h, 1, h)
        first(8 + h, 1, 2, h, f_dn)
    second_dn(1)
    to_partner(0, 1)
    first_wait(2, 3, 2)
    first_wait(3, 3, 3)
    second_up(3)
    to_partner(0, 3)
    permutation()
    for h in range(4):
        first_wait(8 + h, 2, h)
    second_dn(2)
    to_partner(0, 2)
    second_up(1)
    second_dn(0)
    second_up(2)
    second_dn(3)

    ones8 = jnp.ones((8, 128), BF)
    firsts, seconds = (ya, yb), (yb, ya)

    def send1(t, h, k):
        return remote(snd1.at[t, h, k], rcv1.at[t, h, k], r1_send.at[t, h, k], r1_recv.at[t, h, k],
                      at_y(firsts[h]))

    def matmul(t, between=None):
        ext = reps_v[t, :, :, FY:EXT].reshape(256, 128)
        sqr = lax.dot_general(ones8, ext, NT, preferred_element_type=F32)
        for h in range(2):
            sq_buf[y, 2 * t + h] = sqr[:, 128 * h:128 * h + 128]
        if t == 3:
            for k in (1, 0, 2):
                go(sq_buf.at[y], sq_buf.at[y], q_send.at[k], q_recv.at[k], ring[k])

        def tile(m, _):
            d = jnp.where(m == 0, yc, jnp.where(m == 1, ya, jnp.where(m == 2, yb, y)))
            cross = lax.dot_general(
                scen_v[pl.ds(pl.multiple_of(d * 256, 256), 256), :],
                reps_v[t, :, :, 0:FY].reshape(256, FY), NT, preferred_element_type=F32)
            lo, hi = cross[:, :128], cross[:, 128:]
            part[t, 0, m] = lo
            part[t, 1, m] = hi

            @pl.when(m == 0)
            def _():
                snd1[t, 0, 1] = pack(lo, SCALE1)
                send1(t, 0, 1).start()
                snd1[t, 1, 1] = pack(hi, SCALE1)
                send1(t, 1, 1).start()

            @pl.when(m == 1)
            def _():
                snd1[t, 0, 0] = pack(lo, SCALE1)
                send1(t, 0, 0).start()

            @pl.when(m == 2)
            def _():
                snd1[t, 1, 0] = pack(hi, SCALE1)
                send1(t, 1, 0).start()

            return 0

        if between is None:
            lax.fori_loop(0, 4, tile, 0)
        else:
            lax.fori_loop(0, 2, tile, 0)
            between()
            lax.fori_loop(2, 4, tile, 0)
        for h in range(2):
            for k in range(2):
                sends.append(send1(t, h, k))

    def reduce2(t):
        for h in range(2):
            recv(rcv1.at[t, h, 1], r1_send.at[t, h, 1], r1_recv.at[t, h, 1])
            snd2[t, h] = pack(part[t, h, 2 - h] + unpack(rcv1[t, h, 1], SCALE1), SCALE2)
            go(snd2.at[t, h], rcv2.at[t, h], r2_send.at[t, h], r2_recv.at[t, h], at_y(seconds[h]))

    def finish(t, h):
        recv(rcv1.at[t, h, 0], r1_send.at[t, h, 0], r1_recv.at[t, h, 0])
        recv(rcv2.at[t, h], r2_send.at[t, h], r2_recv.at[t, h])
        whole = part[t, h, 3] + unpack(rcv1[t, h, 0], SCALE1) + unpack(rcv2[t, h], SCALE2)
        g = 2 * t + h
        sq_r = sq_buf[0, g] + sq_buf[1, g] + sq_buf[2, g] + sq_buf[3, g]
        return ((sq_s + sq_r[0:1, :]) - 2.0 * whole) * (1.0 / (F * EPS))

    def settle(h, d, value):
        if h == 0:
            cost[(z + d) % 4] = pltpu.roll(value, 32 * x, 1)
        else:
            cost[4 + (x + d) % 4] = pltpu.roll(value, 32 * z, 1)

    partner_wait = lambda t, rs=(0, 1, 2, 3): [from_partner(t, r) for r in rs]

    lax.fori_loop(0, 4, norms, 0)
    partner_wait(0)
    matmul(0)
    arrive_up(0)
    arrive_dn(1)
    arrive_up(3)
    arrive_dn(2)
    lax.fori_loop(4, 8, norms, 0)
    reduce2(0)
    partner_wait(1)
    sq_buf[y, 8] = jnp.concatenate([sqs[k, 0:1, :] for k in range(8)], axis=0)
    matmul(1)
    arrive_up(1)
    arrive_dn(0)
    arrive_up(2)
    arrive_dn(3)
    reduce2(1)
    partner_wait(2)
    matmul(2)
    arrive_far(0)
    arrive_far(1)
    arrive_far(3)
    arrive_far(2)
    partner_wait(3)
    matmul(3, lambda: reduce2(2))
    reduce2(3)
    for k in range(3):
        recv(sq_buf.at[(y + 3 - k) % 4], q_send.at[k], q_recv.at[k])
    sqs[0] = sq_buf[0, 8] + sq_buf[1, 8] + sq_buf[2, 8] + sq_buf[3, 8]
    sq_s = jnp.concatenate(
        [column(sqs[0, pl.ds(2 * y + k, 1), :]) for k in range(2)], axis=0)
    lanes = lax.broadcasted_iota(jnp.int32, (256, 128), 1)
    outer = (lanes < 32) | (lanes >= 96)
    for h in range(2):
        settle(h, 0, finish(0, h))
    for h in range(2):
        keep[h] = finish(1, h)
    for h in range(2):
        one, two = keep[h], finish(2, h)
        settle(h, 3, jnp.where(outer, one, two))
        settle(h, 1, jnp.where(outer, two, one))
    for h in range(2):
        settle(h, 2, finish(3, h))

    def rows_of(q):
        return pi[pl.ds(pl.multiple_of(q * 256, 256), 256), :]

    def col_of(q):
        return pl.ds(pl.multiple_of(q * 256, 256), 256)

    here = col_of(y)

    def permuted(q):
        out = None
        for k in range(3):
            some = lax.dot_general(rows_of(q), split[k], NT, preferred_element_type=F32)
            out = some if out is None else out + some
        return out

    def make_split():
        for g in range(8):
            for k, piece in enumerate(split3(cost[g])):
                split[k, :, 128 * g:128 * g + 128] = piece

    up, dn = ring[0], ring[2]

    v = jnp.zeros((8, 128), F32)
    for it in range(ITERS):
        peak = None
        for g in range(8):
            s = v[g:g + 1, :] - cost[g]
            peak = s if peak is None else jnp.maximum(peak, s)
        peak = jnp.max(peak, axis=1, keepdims=True)
        acc = None
        for g in range(8):
            e = jnp.exp((v[g:g + 1, :] - cost[g]) - peak)
            acc = e if acc is None else acc + e
        u = -math.log(COUNT_S) - (peak + jnp.log(jnp.sum(acc, axis=1, keepdims=True)))
        rows = []
        for g in range(8):
            s = u - cost[g]
            top = jnp.max(s, axis=0, keepdims=True)
            rows.append(top + jnp.log(jnp.sum(jnp.exp(s - top), axis=0, keepdims=True)))
        box1[it] = jnp.concatenate(rows, axis=0)
        for k in NEAR_ORDER:
            go(box1.at[it], in1.at[it, me1], s1.at[it, k], r1.at[it, k], near[k])
        in1[it, me1] = box1[it]
        if it == 0:
            make_split()
            row_snd[0] = permuted((y + 1) % 4)
            go(row_snd.at[0], row_cost.at[:, here], sm.at[0], rm.at[0], up)
            row_snd[1] = permuted((y + 3) % 4)
            go(row_snd.at[1], row_cost.at[:, here], sm.at[1], rm.at[1], dn)
        if it == 1:
            go(row_snd.at[2, 0:128], relay.at[0], sm.at[2], rm.at[2], up)
            go(row_snd.at[2, 128:256], relay.at[1], sm.at[3], rm.at[3], dn)
        if it == ITERS - 1:
            wide = jnp.broadcast_to(u, (256, 128))
            flat = [jnp.transpose(wide[128 * k:128 * k + 128, :])[0:1, :] for k in range(2)]
            u_buf[4] = jnp.concatenate(flat + [jnp.zeros((6, 128), F32)], axis=0)
            u_buf[y] = u_buf[4]
            for k in range(3):
                go(u_buf.at[4], u_buf.at[y], su.at[k], ru.at[k], ring[k])
        for k in range(7):
            recv(in1.at[it, (me1 + 7 - k) % 8], s1.at[it, k], r1.at[it, k])
        box2[it] = lse([in1[it, k] for k in range(8)])
        for k in FAR_ORDER:
            go(box2.at[it], in2.at[it, plane], s2.at[it, k], r2.at[it, k], far[k])
        in2[it, plane] = box2[it]
        if it == 0:
            row_snd[2] = permuted(yc)
            row_cost[:, here] = permuted(y)
            flush()
        if it == 1:
            recv(relay.at[0], sm.at[2], rm.at[2])
            go(relay.at[0], row_cost.at[0:128, col_of((y + 3) % 4)], sm.at[4], rm.at[4], up)
            recv(relay.at[1], sm.at[3], rm.at[3])
            go(relay.at[1], row_cost.at[128:256, col_of((y + 1) % 4)], sm.at[5], rm.at[5], dn)
        if it == ITERS - 1:
            for k in range(3):
                recv(u_buf.at[(y + 3 - k) % 4], su.at[k], ru.at[k])
            recv(row_cost.at[:, col_of((y + 3) % 4)], sm.at[0], rm.at[0])
            recv(row_cost.at[:, col_of((y + 1) % 4)], sm.at[1], rm.at[1])
            recv(row_cost.at[0:128, col_of(yc)], sm.at[4], rm.at[4])
            recv(row_cost.at[128:256, col_of(yc)], sm.at[5], rm.at[5])
            u_ref[...] = jnp.concatenate([u_buf[k, 0:2, :] for k in range(4)], axis=0)
            flush()
        for k in range(15):
            recv(in2.at[it, (plane + 15 - k) % 16], s2.at[it, k], r2.at[it, k])
        v = -math.log(COUNT_R) - lse([in2[it, k] for k in range(16)])

    flat = jnp.concatenate([v[g:g + 1, :] for g in range(8)], axis=1)
    pieces = split3(flat)
    row = lax.broadcasted_iota(jnp.int32, (8, 1024), 0)
    three = jnp.where(row == 0, pieces[0].astype(F32),
                      jnp.where(row == 1, pieces[1].astype(F32),
                                jnp.where(row == 2, pieces[2].astype(F32), 0.0))).astype(BF)
    got = lax.dot_general(three, rows_of(y), NT, preferred_element_type=F32)
    v_ref[...] = got[0:1, :] + got[1:2, :] + got[2:3, :]
    flush()


VM = pl.BlockSpec(memory_space=pltpu.VMEM)
ANY = pl.BlockSpec(memory_space=pl.ANY)


def emit(u_ref, v_ref, cost_ref, u_out, v_out, mem_out, u_buf, v_buf, m_buf, sem):
    u_buf[...] = u_ref[...] * EPS
    v_buf[...] = v_ref[...] * EPS
    copies = [pltpu.make_async_copy(u_buf, u_out, sem.at[0]),
              pltpu.make_async_copy(v_buf, v_out, sem.at[1])]
    for cp in copies:
        cp.start()
    for h in range(2):
        half = slice(128 * h, 128 * h + 128)
        v_col = column(v_ref[:, half])
        for k in range(8):
            cols = slice(128 * k, 128 * k + 128)
            m_buf[half, cols] = (
                COUNT_S * jnp.exp((u_ref[k:k + 1, :] + v_col) - cost_ref[half, cols])).astype(BF)
        cp = pltpu.make_async_copy(m_buf.at[half], mem_out.at[half], sem.at[2 + h])
        cp.start()
        copies.append(cp)
    for cp in copies:
        cp.wait()


def on_device(scenarios, rep_index):
    dma = pltpu.SemaphoreType.DMA
    shapes = (jax.ShapeDtypeStruct((8, 128), F32),
              jax.ShapeDtypeStruct((1, 256), F32),
              jax.ShapeDtypeStruct((256, 1024), BF))
    results = pl.pallas_call(
        kernel,
        out_shape=shapes[:2] + (jax.ShapeDtypeStruct((256, 1024), F32),),
        in_specs=[pl.BlockSpec(memory_space=pltpu.HBM)] * 2,
        out_specs=(VM, VM, VM),
        scratch_shapes=[
            pltpu.VMEM((ROWS, FY), BF),
            pltpu.VMEM((4, 2, 128, EXT), BF),
            pltpu.VMEM((4, 2, 4, 256, 128), F32),
            pltpu.VMEM((4, 2, 2, 192, 128), jnp.int32),
            pltpu.VMEM((4, 2, 2, 192, 128), jnp.int32),
            pltpu.VMEM((4, 2, 192, 128), jnp.int32),
            pltpu.VMEM((4, 2, 192, 128), jnp.int32),
            pltpu.VMEM((8, 8, 128), F32),
            pltpu.VMEM((8, 256, 128), F32),
            pltpu.VMEM((1, 1024), jnp.int32),
            pltpu.VMEM((1024, 1024), BF),
            pltpu.VMEM((4, 9, 8, 128), F32),
            pltpu.VMEM((5, 8, 128), F32),
            pltpu.VMEM((3, 8, 8, 128), F32),
            pltpu.VMEM((3, 16, 8, 128), F32),
            pltpu.VMEM((3, 8, 128), F32),
            pltpu.VMEM((3, 8, 128), F32),
            pltpu.VMEM((2, 256, 128), F32),
            pltpu.VMEM((3, 256, 1024), BF),
            pltpu.VMEM((3, 256, 256), F32),
            pltpu.VMEM((2, 128, 256), F32),
            dma((5,)), dma((12,)), dma((12,)), dma((3, 4)), dma((3, 4)), dma((4, 4)), dma((4, 4)),
            dma((4, 2, 2)), dma((4, 2, 2)), dma((4, 2)), dma((4, 2)), dma((3,)), dma((3,)),
            dma((3, 7)), dma((3, 7)), dma((3, 15)), dma((3, 15)), dma((3,)), dma((3,)),
            dma((6,)), dma((6,)),
        ],
        compiler_params=pltpu.CompilerParams(
            collective_id=0, has_side_effects=True, vmem_limit_bytes=50 << 20),
        name="transport",
    )(pltpu.with_memory_space_constraint(rep_index.reshape(1, 1024), pltpu.HBM), scenarios)
    u, v, member = pl.pallas_call(
        emit,
        out_shape=shapes,
        in_specs=[VM] * 3,
        out_specs=(ANY, ANY, ANY),
        scratch_shapes=[pltpu.VMEM((8, 128), F32), pltpu.VMEM((1, 256), F32),
                        pltpu.VMEM((256, 1024), BF), dma((4,))],
        compiler_params=pltpu.CompilerParams(vmem_limit_bytes=4 << 20),
        name="emit",
    )(*results)
    return u.reshape(1024), v.reshape(256), member


def solution(mesh):
    return jax.shard_map(
        on_device,
        mesh=mesh,
        in_specs=(P("scen", "rep"), P()),
        out_specs=(P("scen"), P("rep"), P("rep", "scen")),
        check_vma=False,
    )
```

```python
import functools
import math

import jax
import jax.numpy as jnp
from jax import lax
from jax.experimental import pallas as pl
from jax.experimental.pallas import tpu as pltpu
from jax.sharding import PartitionSpec as P

F = 16384
ITERS = 3
COUNT_S = 32768
COUNT_R = 1024
EPS = 0.1
FY = 4096
ROWS = 1024
EXT = FY + 128
QUARTERS = ((0, 1024), (1024, 2048), (2048, 3072), (3072, EXT))
MESH = pl.DeviceIdType.MESH
BF = jnp.bfloat16
F32 = jnp.float32
NT = (((1,), (1,)), ((), ()))


def remote(src, dst, ssem, rsem, dev):
    return pltpu.make_async_remote_copy(
        src_ref=src, dst_ref=dst, send_sem=ssem, recv_sem=rsem, device_id=dev, device_id_type=MESH
    )


def place():
    scen = lax.axis_index("scen")
    y = lax.axis_index("rep")
    return scen // 8, (scen // 2) % 4, scen % 2, y


def dev(x, z, c, y):
    return ((x * 4 + z) * 2 + c, y)


def greet(peers):
    sem = pltpu.get_barrier_semaphore()
    for p in peers:
        pl.semaphore_signal(sem, inc=1, device_id=p, device_id_type=MESH)


def meet(count):
    pl.semaphore_wait(pltpu.get_barrier_semaphore(), count)


def column(row):
    return jnp.transpose(jnp.broadcast_to(row, (128, 128)))


def split3(v):
    hi = v.astype(BF)
    rest = v - hi.astype(F32)
    mid = rest.astype(BF)
    low = (rest - mid.astype(F32)).astype(BF)
    return hi, mid, low


def pack(x, scale):
    q = [jnp.round(x[64 * k:64 * k + 64] * scale).astype(jnp.int32) for k in range(4)]
    return jnp.concatenate(
        [(q[k] << 8) | ((q[3] >> (8 * k)) & 255) for k in range(3)], axis=0)


def unpack(w, scale):
    w = [w[64 * k:64 * k + 64] for k in range(3)]
    last = ((w[2] << 24) >> 8) | ((w[1] & 255) << 8) | (w[0] & 255)
    q = [w[0] >> 8, w[1] >> 8, w[2] >> 8, last]
    return jnp.concatenate(q, axis=0).astype(F32) * (1.0 / scale)


SPOT = {
    "O0": (0, 0), "O1": (0, 1), "U0": (0, 2), "O3": (0, 3),
    "D0": (1, 0), "D1": (1, 1), "O2": (1, 2), "U3": (1, 3),
    "F0": (2, 0), "U1": (2, 1), "U2": (2, 2), "D3": (2, 3),
    "D2": (3, 0), "F1": (3, 1), "F2": (3, 2), "F3": (3, 3),
}
NEAR_ORDER = (3, 4, 2, 5, 1, 6, 0)
FAR_ORDER = tuple(sorted(range(15), key=lambda k: -(min((k + 1) % 4, 4 - (k + 1) % 4)
                                                   + min((k + 1) // 4, 4 - (k + 1) // 4))))
SCALE1 = 3.5
SCALE2 = 1.75


def lse(rows):
    peak = functools.reduce(jnp.maximum, rows)
    return peak + jnp.log(functools.reduce(jnp.add, [jnp.exp(r - peak) for r in rows]))


def kernel(rep_hbm, scen_hbm, u_ref, v_ref, row_cost,
           scen_v, reps_v, part, snd1, rcv1, snd2, rcv2, sqs, cost, rep_v, pi, sq_buf,
           u_buf, in1, in2, box1, box2, keep, split, row_snd, relay, u_out, v_out,
           hbm_sem, f_send, f_recv, s_send, s_recv, c_send, c_recv, r1_send, r1_recv,
           r2_send, r2_recv, q_send, q_recv, s1, r1, s2, r2, su, ru, sm, rm):
    x, z, c, y = place()
    pf = x * (1 - c) + z * c
    ps = z * (1 - c) + x * c

    def along_first(d):
        return dev((x + (1 - c) * d) % 4, (z + c * d) % 4, c, y)

    def along_second(d):
        return dev((x + c * d) % 4, (z + (1 - c) * d) % 4, c, y)

    f_up, f_dn = along_first(1), along_first(3)
    s_up, s_dn = along_second(1), along_second(3)
    partner = dev(x, z, 1 - c, y)
    ya = y + 1 - 2 * (y % 2)
    yb = 3 - y
    yc = (y + 2) % 4
    at_y = lambda q: dev(x, z, c, q)
    plane = x * 4 + z
    me1 = y * 2 + c
    near, far = [], []
    for k in range(1, 8):
        q = (me1 + k) % 8
        near.append(dev(x, z, q % 2, q // 2))
    for k in range(1, 16):
        q = (plane + k) % 16
        far.append(dev(q // 4, q % 4, c, y))
    ring = [at_y((y + k) % 4) for k in range(1, 4)]

    rep_load = pltpu.make_async_copy(rep_hbm, rep_v, hbm_sem.at[4])
    rep_load.start()
    loads = []
    for k in range(4):
        cols = pl.ds(k * 1024, 1024)
        cp = pltpu.make_async_copy(scen_hbm.at[:, cols], scen_v.at[:, cols], hbm_sem.at[k])
        cp.start()
        loads.append(cp)
    greet([f_up, f_dn, s_up, s_dn, partner, at_y(ya), at_y(yb)])
    rep_load.wait()

    rep_i = rep_v[...]
    rep_f = rep_i.astype(F32)
    counts = []
    cols_f = [column(rep_f[:, 128 * k:128 * k + 128]) for k in range(8)]
    for g in range(8):
        row = rep_f[:, 128 * g:128 * g + 128]
        acc = jnp.zeros((128, 128), F32)
        for k in range(8):
            acc = acc + jnp.where(cols_f[k] < row, 1.0, 0.0)
        counts.append(jnp.sum(acc, axis=0, keepdims=True))
    rank = jnp.concatenate(counts, axis=1)
    rank_i = rank.astype(jnp.int32)
    blk_i = rep_i >> 10
    bx, bz, bc = blk_i >> 3, (blk_i >> 1) & 3, blk_i & 1
    slot = jnp.where(bc == 0, bz * 4 + bx, 16 + bx * 4 + bz)
    prow = (32 * slot + rank_i - 32 * blk_i).astype(F32)

    mine = (lax.axis_index("scen")).astype(F32)
    jot = lax.broadcasted_iota(jnp.int32, (32, ROWS), 0).astype(F32)
    hit = (rank - 32.0 * mine) == jot
    pos = jnp.sum(jnp.where(hit, rep_f, 0.0), axis=1, keepdims=True) - 1024.0 * mine
    sel = jnp.where(
        lax.broadcasted_iota(jnp.int32, (32, ROWS), 1).astype(F32) == pos, 1.0, 0.0
    ).astype(BF)

    def blk(name, cc, lo=0, hi=EXT):
        t, k = SPOT[name]
        return reps_v.at[t, cc, pl.ds(32 * k, 32), pl.ds(lo, hi - lo)]

    def go(src, dst, ssem, rsem, to):
        remote(src, dst, ssem, rsem, to).start()

    def recv(buf, rsem):
        remote(buf, buf, f_send.at[0], rsem, partner).wait_recv()

    def sent(buf, ssem):
        remote(buf, buf, ssem, f_recv.at[0], partner).wait_send()

    def first(i, name, there, h, to):
        go(blk(name, c, *QUARTERS[h]), blk(there, c, *QUARTERS[h]), f_send.at[0], f_recv.at[i], to)

    def first_wait(i, name, lo, hi):
        recv(blk(name, c, lo, hi), f_recv.at[i])

    total = jnp.zeros((32, 1), F32)
    for k in range(4):
        loads[k].wait()
        cols = slice(k * 1024, (k + 1) * 1024)
        own = jnp.dot(sel, scen_v[:, cols], preferred_element_type=F32)
        reps_v[0, c, 0:32, cols] = own.astype(BF)
        total = total + jnp.sum(own * own, axis=1, keepdims=True)
        if k == 0:
            meet(7)
        if k < 3:
            first(min(k, 2), "O0", "O3", k, f_up)
            first(3 if k < 2 else 2 + k, "O0", "O1", k, f_dn)
    hi, mid, low = split3(total)
    lane = lax.broadcasted_iota(jnp.int32, (32, 128), 1)
    ext = jnp.where(lane == 0, hi.astype(F32),
                    jnp.where(lane == 1, mid.astype(F32),
                              jnp.where(lane == 2, low.astype(F32), 0.0)))
    reps_v[0, c, 0:32, FY:EXT] = ext.astype(BF)
    first(2, "O0", "O3", 3, f_up)
    first(5, "O0", "O1", 3, f_dn)

    def to_partner(name):
        t, _ = SPOT[name]
        go(blk(name, c), blk(name, c), c_send.at[t], c_recv.at[t], partner)

    def from_partner(t):
        recv(reps_v.at[t, 1 - c], c_recv.at[t])

    def second(r, up):
        i, there, to = (0, "U%d" % r, s_up) if up else (1, "D%d" % r, s_dn)
        go(blk("O%d" % r, c), blk(there, c), s_send.at[0], s_recv.at[i, r], to)

    def arrive(name):
        group, r = name[0], int(name[1])
        recv(blk(name, c), s_recv.at["UDF".index(group), r])
        if name in ("U0", "U3", "D1", "D2"):
            go(blk(name, c), blk("F%d" % r, c), s_send.at[0], s_recv.at[2, r],
               s_up if group == "U" else s_dn)
        to_partner(name)

    second(0, True)
    second(0, False)
    to_partner("O0")

    def norms(i, _):
        rows = pl.ds(pl.multiple_of(i * 128, 128), 128)
        acc = jnp.zeros((128, 128), F32)
        for k in range(32):
            v = scen_v[rows, k * 128:(k + 1) * 128].astype(F32)
            acc = acc + v * v
        wide = jnp.broadcast_to(jnp.sum(acc, axis=1, keepdims=True), (128, 128))
        sqs[i] = jnp.transpose(wide)[0:8, :]
        return 0

    def permutation():
        for k in range(8):
            col = column(prow[:, 128 * k:128 * k + 128])
            for g in range(8):
                lane = lax.broadcasted_iota(jnp.int32, (128, 128), 1).astype(F32) + 128.0 * g
                pi[128 * k:128 * k + 128, 128 * g:128 * g + 128] = jnp.where(
                    col == lane, 1.0, 0.0).astype(BF)

    for h in range(2):
        first_wait(h, "O3", *QUARTERS[h])
        first(6, "O3", "O2", h, f_up)
    first_wait(3, "O1", 0, 2048)
    for h in range(2, 4):
        first_wait(2 + h, "O1", *QUARTERS[h])
        first(6, "O1", "O2", h, f_dn)
    second(1, False)
    to_partner("O1")
    first_wait(2, "O3", 2048, EXT)
    second(3, True)
    to_partner("O3")
    arrive("U0")
    second(1, True)
    second(3, False)

    ones8 = jnp.ones((8, 128), BF)
    firsts, seconds = (ya, yb), (yb, ya)

    def send1(t, h, k):
        return remote(snd1.at[t, k, h], rcv1.at[t, k, h], r1_send.at[0], r1_recv.at[t, k],
                      at_y(firsts[h]))

    def matmul(t, after=()):
        ext = reps_v[t, :, :, FY:EXT].reshape(256, 128)
        sqr = lax.dot_general(ones8, ext, NT, preferred_element_type=F32)
        for h in range(2):
            sq_buf[y, 2 * t + h] = sqr[:, 128 * h:128 * h + 128]
        if t == 3:
            for k in (1, 0, 2):
                go(sq_buf.at[y], sq_buf.at[y], q_send.at[0], q_recv.at[0], ring[k])

        def tile(m, _):
            d = jnp.where(m == 0, yc, jnp.where(m == 1, ya, jnp.where(m == 2, yb, y)))
            cross = lax.dot_general(
                scen_v[pl.ds(pl.multiple_of(d * 256, 256), 256), :],
                reps_v[t, :, :, 0:FY].reshape(256, FY), NT, preferred_element_type=F32)
            lo, hi = cross[:, :128], cross[:, 128:]
            part[t, 0, m] = lo
            part[t, 1, m] = hi

            @pl.when(m == 0)
            def _():
                snd1[t, 1, 0] = pack(lo, SCALE1)
                send1(t, 0, 1).start()
                snd1[t, 1, 1] = pack(hi, SCALE1)
                send1(t, 1, 1).start()

            @pl.when(m == 1)
            def _():
                snd1[t, 0, 0] = pack(lo, SCALE1)
                send1(t, 0, 0).start()

            @pl.when(m == 2)
            def _():
                snd1[t, 0, 1] = pack(hi, SCALE1)
                send1(t, 1, 0).start()

            for k, act in enumerate(after):
                pl.when(m == k)(act)
            return 0

        lax.fori_loop(0, 4, tile, 0)

    def reduce2(t):
        recv(rcv1.at[t, 1], r1_recv.at[t, 1])
        for h in range(2):
            snd2[t, h] = pack(part[t, h, 2 - h] + unpack(rcv1[t, 1, h], SCALE1), SCALE2)
            go(snd2.at[t, h], rcv2.at[t, h], r2_send.at[0], r2_recv.at[t], at_y(seconds[h]))

    def finish(t, h):
        if h == 0:
            recv(rcv1.at[t, 0], r1_recv.at[t, 0])
            recv(rcv2.at[t], r2_recv.at[t])
        whole = part[t, h, 3] + unpack(rcv1[t, 0, h], SCALE1) + unpack(rcv2[t, h], SCALE2)
        g = 2 * t + h
        sq_r = sq_buf[0, g] + sq_buf[1, g] + sq_buf[2, g] + sq_buf[3, g]
        return ((sq_s + sq_r[0:1, :]) - 2.0 * whole) * (1.0 / (F * EPS))

    def settle(h, d, value):
        if h == 0:
            cost[(z + d) % 4] = pltpu.roll(value, 32 * x, 1)
        else:
            cost[4 + (x + d) % 4] = pltpu.roll(value, 32 * z, 1)

    def far_along():
        first_wait(6, "O2", 0, EXT)
        second(2, True)
        second(2, False)
        to_partner("O2")

    def acts(*names):
        def act():
            for name in names:
                far_along() if name == "O2" else arrive(name)
        return act

    lax.fori_loop(0, 4, norms, 0)
    from_partner(0)
    matmul(0, (acts("D0"), acts("O2"), acts(), acts("D1")))
    arrive("U3")
    lax.fori_loop(4, 8, norms, 0)
    reduce2(0)
    from_partner(1)
    sq_buf[y, 8] = jnp.concatenate([sqs[k, 0:1, :] for k in range(8)], axis=0)
    matmul(1, (acts(), acts(), acts("F0"), acts("U1", "D3")))
    arrive("D2")
    arrive("U2")
    reduce2(1)
    from_partner(2)
    matmul(2, (acts(), acts("F1"), acts(), acts("F3")))
    arrive("F2")
    permutation()
    from_partner(3)
    matmul(3, (lambda: reduce2(2),))
    reduce2(3)
    recv(sq_buf.at[0:3], q_recv.at[0])
    sqs[0] = sq_buf[0, 8] + sq_buf[1, 8] + sq_buf[2, 8] + sq_buf[3, 8]
    sq_s = jnp.concatenate(
        [column(sqs[0, pl.ds(2 * y + k, 1), :]) for k in range(2)], axis=0)
    place_of = lax.broadcasted_iota(jnp.int32, (256, 128), 1) // 32
    for t in range(3):
        for h in range(2):
            keep[t, h] = finish(t, h)
            if t == 1:
                settle(h, 0, jnp.where(place_of == 2, keep[1, h], keep[0, h]))
            if t == 2:
                moved = pltpu.roll(keep[0, h], 64, 1)
                settle(h, 3, jnp.where(place_of == 0, moved,
                                       jnp.where(place_of == 3, keep[1, h], keep[2, h])))
    for h in range(2):
        last = finish(3, h)
        settle(h, 1, jnp.where(place_of < 2, keep[1, h],
                               jnp.where(place_of == 2, pltpu.roll(last, 64, 1), keep[2, h])))
        settle(h, 2, jnp.where(place_of == 0, keep[2, h], last))

    def rows_of(q):
        return pi[pl.ds(pl.multiple_of(q * 256, 256), 256), :]

    def col_of(q):
        return pl.ds(pl.multiple_of(q * 256, 256), 256)

    here = col_of(y)

    def permuted(q):
        out = None
        for k in range(3):
            some = lax.dot_general(rows_of(q), split[k], NT, preferred_element_type=F32)
            out = some if out is None else out + some
        return out

    def make_split():
        for g in range(8):
            for k, piece in enumerate(split3(cost[g])):
                split[k, :, 128 * g:128 * g + 128] = piece

    up, dn = ring[0], ring[2]
    cuts = ((0, 96), (96, 96), (192, 64))

    def row_piece(n):
        rows = pl.ds(*cuts[n])
        for k, to in ((0, up), (1, dn)):
            go(row_snd.at[k, rows], row_cost.at[rows, here], sm.at[0], rm.at[3], to)

    v = jnp.zeros((8, 128), F32)
    for it in range(ITERS):
        peak = None
        for g in range(8):
            s = v[g:g + 1, :] - cost[g]
            peak = s if peak is None else jnp.maximum(peak, s)
        peak = jnp.max(peak, axis=1, keepdims=True)
        acc = None
        for g in range(8):
            e = jnp.exp((v[g:g + 1, :] - cost[g]) - peak)
            acc = e if acc is None else acc + e
        u = -math.log(COUNT_S) - (peak + jnp.log(jnp.sum(acc, axis=1, keepdims=True)))
        rows = []
        for g in range(8):
            s = u - cost[g]
            top = jnp.max(s, axis=0, keepdims=True)
            rows.append(top + jnp.log(jnp.sum(jnp.exp(s - top), axis=0, keepdims=True)))
        box1[it] = jnp.concatenate(rows, axis=0)
        for k in NEAR_ORDER:
            go(box1.at[it], in1.at[it, me1], s1.at[it], r1.at[it], near[k])
        in1[it, me1] = box1[it]
        if it == 0:
            make_split()
            row_snd[2] = permuted(yc)
            row_snd[0] = permuted((y + 1) % 4)
        if it == ITERS - 1:
            wide = jnp.broadcast_to(u, (256, 128))
            flat = [jnp.transpose(wide[128 * k:128 * k + 128, :])[0:1, :] for k in range(2)]
            u_buf[4] = jnp.concatenate(flat + [jnp.zeros((6, 128), F32)], axis=0)
            u_buf[y] = u_buf[4]
            for k in range(3):
                go(u_buf.at[4], u_buf.at[y], su.at[0], ru.at[0], ring[k])
        recv(in1.at[it, 0:7], r1.at[it])
        box2[it] = lse([in1[it, k] for k in range(8)])
        for k in FAR_ORDER:
            go(box2.at[it], in2.at[it, plane], s2.at[it], r2.at[it], far[k])
        in2[it, plane] = box2[it]
        if it == 0:
            go(row_snd.at[2, 0:128], relay.at[0], sm.at[0], rm.at[0], up)
            go(row_snd.at[2, 128:256], relay.at[1], sm.at[0], rm.at[1], dn)
            row_snd[1] = permuted((y + 3) % 4)
            row_piece(0)
            row_snd[3] = permuted(y)
            kept = pltpu.make_async_copy(row_snd.at[3], row_cost.at[:, here], hbm_sem.at[4])
            kept.start()
        if it == 1:
            recv(relay.at[0], rm.at[0])
            go(relay.at[0], row_cost.at[0:128, col_of((y + 3) % 4)], sm.at[0], rm.at[2], up)
            recv(relay.at[1], rm.at[1])
            go(relay.at[1], row_cost.at[128:256, col_of((y + 1) % 4)], sm.at[0], rm.at[2], dn)
            row_piece(1)
        if it == ITERS - 1:
            recv(u_buf.at[0:3], ru.at[0])
            row_piece(2)
            recv(row_cost.at[:, col_of(yc)], rm.at[2])
            kept.wait()
            u_out[...] = jnp.concatenate([u_buf[k, 0:2, :] for k in range(4)], axis=0)
            u_copy = pltpu.make_async_copy(u_out, u_ref, hbm_sem.at[0])
            u_copy.start()
            sent(reps_v.at[0, c, 0:96], f_send.at[0])
            sent(reps_v.at[0:3, c], s_send.at[0])
            for t in range(4):
                sent(reps_v.at[t, c], c_send.at[t])
            sent(snd1, r1_send.at[0])
            sent(snd2, r2_send.at[0])
            sent(sq_buf.at[0:3], q_send.at[0])
        recv(in2.at[it, 0:15], r2.at[it])
        sent(in1.at[it, 0:7], s1.at[it])
        sent(in2.at[it, 0:15], s2.at[it])
        v = -math.log(COUNT_R) - lse([in2[it, k] for k in range(16)])

    flat = jnp.concatenate([v[g:g + 1, :] for g in range(8)], axis=1)
    pieces = split3(flat)
    row = lax.broadcasted_iota(jnp.int32, (8, 1024), 0)
    three = jnp.where(row == 0, pieces[0].astype(F32),
                      jnp.where(row == 1, pieces[1].astype(F32),
                                jnp.where(row == 2, pieces[2].astype(F32), 0.0))).astype(BF)
    got = lax.dot_general(three, rows_of(y), NT, preferred_element_type=F32)
    v_out[...] = got[0:1, :] + got[1:2, :] + got[2:3, :]
    v_copy = pltpu.make_async_copy(v_out, v_ref, hbm_sem.at[1])
    v_copy.start()
    recv(row_cost.at[:, 0:512], rm.at[3])
    sent(row_snd, sm.at[0])
    sent(u_buf.at[0:3], su.at[0])
    u_copy.wait()
    v_copy.wait()


VM = pl.BlockSpec(memory_space=pltpu.VMEM)
ANY = pl.BlockSpec(memory_space=pl.ANY)


def emit(u_ref, v_ref, cost_ref, u_out, v_out, mem_out, u_buf, v_buf, m_buf, sem):
    u_buf[...] = u_ref[...] * EPS
    v_buf[...] = v_ref[...] * EPS
    copies = [pltpu.make_async_copy(u_buf, u_out, sem.at[0]),
              pltpu.make_async_copy(v_buf, v_out, sem.at[1])]
    for cp in copies:
        cp.start()
    for h in range(2):
        half = slice(128 * h, 128 * h + 128)
        v_col = column(v_ref[:, half])
        for k in range(8):
            cols = slice(128 * k, 128 * k + 128)
            m_buf[half, cols] = (
                COUNT_S * jnp.exp((u_ref[k:k + 1, :] + v_col) - cost_ref[half, cols])).astype(BF)
        cp = pltpu.make_async_copy(m_buf.at[half], mem_out.at[half], sem.at[2 + h])
        cp.start()
        copies.append(cp)
    for cp in copies:
        cp.wait()


def on_device(scenarios, rep_index):
    dma = pltpu.SemaphoreType.DMA
    shapes = (jax.ShapeDtypeStruct((8, 128), F32),
              jax.ShapeDtypeStruct((1, 256), F32),
              jax.ShapeDtypeStruct((256, 1024), BF))
    results = pl.pallas_call(
        kernel,
        out_shape=shapes[:2] + (jax.ShapeDtypeStruct((256, 1024), F32),),
        in_specs=[pl.BlockSpec(memory_space=pltpu.HBM)] * 2,
        out_specs=(ANY, ANY, ANY),
        scratch_shapes=[
            pltpu.VMEM((ROWS, FY), BF),
            pltpu.VMEM((4, 2, 128, EXT), BF),
            pltpu.VMEM((4, 2, 4, 256, 128), F32),
            pltpu.VMEM((4, 2, 2, 192, 128), jnp.int32),
            pltpu.VMEM((4, 2, 2, 192, 128), jnp.int32),
            pltpu.VMEM((4, 2, 192, 128), jnp.int32),
            pltpu.VMEM((4, 2, 192, 128), jnp.int32),
            pltpu.VMEM((8, 8, 128), F32),
            pltpu.VMEM((8, 256, 128), F32),
            pltpu.VMEM((1, 1024), jnp.int32),
            pltpu.VMEM((1024, 1024), BF),
            pltpu.VMEM((4, 9, 8, 128), F32),
            pltpu.VMEM((5, 8, 128), F32),
            pltpu.VMEM((3, 8, 8, 128), F32),
            pltpu.VMEM((3, 16, 8, 128), F32),
            pltpu.VMEM((3, 8, 128), F32),
            pltpu.VMEM((3, 8, 128), F32),
            pltpu.VMEM((3, 2, 256, 128), F32),
            pltpu.VMEM((3, 256, 1024), BF),
            pltpu.VMEM((4, 256, 256), F32),
            pltpu.VMEM((2, 128, 256), F32),
            pltpu.VMEM((8, 128), F32),
            pltpu.VMEM((1, 256), F32),
            dma((5,)), dma((1,)), dma((7,)), dma((1,)), dma((3, 4)), dma((4,)), dma((4,)),
            dma((1,)), dma((4, 2)), dma((1,)), dma((4,)), dma((1,)), dma((1,)),
            dma((3,)), dma((3,)), dma((3,)), dma((3,)), dma((1,)), dma((1,)),
            dma((1,)), dma((4,)),
        ],
        compiler_params=pltpu.CompilerParams(
            collective_id=0, has_side_effects=True, vmem_limit_bytes=50 << 20),
        name="transport",
    )(pltpu.with_memory_space_constraint(rep_index.reshape(1, 1024), pltpu.HBM), scenarios)
    u, v, member = pl.pallas_call(
        emit,
        out_shape=shapes,
        in_specs=[VM] * 3,
        out_specs=(ANY, ANY, ANY),
        scratch_shapes=[pltpu.VMEM((8, 128), F32), pltpu.VMEM((1, 256), F32),
                        pltpu.VMEM((256, 1024), BF), dma((4,))],
        compiler_params=pltpu.CompilerParams(vmem_limit_bytes=4 << 20),
        name="emit",
    )(*results)
    return u.reshape(1024), v.reshape(256), member


def solution(mesh):
    return jax.shard_map(
        on_device,
        mesh=mesh,
        in_specs=(P("scen", "rep"), P()),
        out_specs=(P("scen"), P("rep"), P("rep", "scen")),
        check_vma=False,
    )
```

```python
import functools
import math

import jax
import jax.numpy as jnp
from jax import lax
from jax.experimental import pallas as pl
from jax.experimental.pallas import tpu as pltpu
from jax.sharding import PartitionSpec as P

F = 16384
ITERS = 3
COUNT_S = 32768
COUNT_R = 1024
EPS = 0.1
FY = 4096
ROWS = 1024
EXT = FY + 128
QUARTERS = ((0, 1024), (1024, 2048), (2048, 3072), (3072, EXT))
MESH = pl.DeviceIdType.MESH
BF = jnp.bfloat16
F32 = jnp.float32
NT = (((1,), (1,)), ((), ()))


def remote(src, dst, ssem, rsem, dev):
    return pltpu.make_async_remote_copy(
        src_ref=src, dst_ref=dst, send_sem=ssem, recv_sem=rsem, device_id=dev, device_id_type=MESH
    )


def place():
    scen = lax.axis_index("scen")
    y = lax.axis_index("rep")
    return scen // 8, (scen // 2) % 4, scen % 2, y


def dev(x, z, c, y):
    return ((x * 4 + z) * 2 + c, y)


def greet(peers):
    sem = pltpu.get_barrier_semaphore()
    for p in peers:
        pl.semaphore_signal(sem, inc=1, device_id=p, device_id_type=MESH)


def meet(count):
    pl.semaphore_wait(pltpu.get_barrier_semaphore(), count)


def column(row):
    return jnp.transpose(jnp.broadcast_to(row, (128, 128)))


def split3(v):
    hi = v.astype(BF)
    rest = v - hi.astype(F32)
    mid = rest.astype(BF)
    low = (rest - mid.astype(F32)).astype(BF)
    return hi, mid, low


def pack(x, scale):
    q = [jnp.round(x[64 * k:64 * k + 64] * scale).astype(jnp.int32) for k in range(4)]
    return jnp.concatenate(
        [(q[k] << 8) | ((q[3] >> (8 * k)) & 255) for k in range(3)], axis=0)


def unpack(w, scale):
    w = [w[64 * k:64 * k + 64] for k in range(3)]
    last = ((w[2] << 24) >> 8) | ((w[1] & 255) << 8) | (w[0] & 255)
    q = [w[0] >> 8, w[1] >> 8, w[2] >> 8, last]
    return jnp.concatenate(q, axis=0).astype(F32) * (1.0 / scale)


SPOT = {
    "O0": (0, 0), "O1": (0, 1), "U0": (0, 2), "O3": (0, 3),
    "D0": (1, 0), "D1": (1, 1), "O2": (1, 2), "U3": (1, 3),
    "F0": (2, 0), "U1": (2, 1), "D2": (2, 2), "D3": (2, 3),
    "U2": (3, 0), "F1": (3, 1), "F2": (3, 2), "F3": (3, 3),
}
NEAR_ORDER = (3, 4, 2, 5, 1, 6, 0)
FAR_ORDER = tuple(sorted(range(15), key=lambda k: -(min((k + 1) % 4, 4 - (k + 1) % 4)
                                                   + min((k + 1) // 4, 4 - (k + 1) // 4))))
SCALE1 = 3.5
SCALE2 = 1.75


def lse(rows):
    peak = functools.reduce(jnp.maximum, rows)
    return peak + jnp.log(functools.reduce(jnp.add, [jnp.exp(r - peak) for r in rows]))


def kernel(rep_hbm, scen_hbm, u_ref, v_ref, row_cost,
           scen_v, reps_v, part, snd1, rcv1, snd2, rcv2, sqs, cost, rep_v, pi, sq_buf,
           u_buf, in1, in2, box1, box2, keep, split, row_snd, relay, u_out, v_out,
           hbm_sem, f_send, f_recv, s_send, s_recv, c_send, c_recv, r1_send, r1_recv,
           r2_send, r2_recv, q_send, q_recv, s1, r1, s2, r2, su, ru, sm, rm):
    x, z, c, y = place()
    pf = x * (1 - c) + z * c
    ps = z * (1 - c) + x * c

    def along_first(d):
        return dev((x + (1 - c) * d) % 4, (z + c * d) % 4, c, y)

    def along_second(d):
        return dev((x + c * d) % 4, (z + (1 - c) * d) % 4, c, y)

    f_up, f_dn = along_first(1), along_first(3)
    s_up, s_dn = along_second(1), along_second(3)
    partner = dev(x, z, 1 - c, y)
    ya = y + 1 - 2 * (y % 2)
    yb = 3 - y
    yc = (y + 2) % 4
    at_y = lambda q: dev(x, z, c, q)
    plane = x * 4 + z
    me1 = y * 2 + c
    near, far = [], []
    for k in range(1, 8):
        q = (me1 + k) % 8
        near.append(dev(x, z, q % 2, q // 2))
    for k in range(1, 16):
        q = (plane + k) % 16
        far.append(dev(q // 4, q % 4, c, y))
    ring = [at_y((y + k) % 4) for k in range(1, 4)]

    rep_load = pltpu.make_async_copy(rep_hbm, rep_v, hbm_sem.at[4])
    rep_load.start()
    loads = []
    for k in range(4):
        cols = pl.ds(k * 1024, 1024)
        cp = pltpu.make_async_copy(scen_hbm.at[:, cols], scen_v.at[:, cols], hbm_sem.at[k])
        cp.start()
        loads.append(cp)
    greet([f_up, f_dn, s_up, s_dn, partner, at_y(ya), at_y(yb)])
    rep_load.wait()

    rep_i = rep_v[...]
    rep_f = rep_i.astype(F32)
    counts = []
    cols_f = [column(rep_f[:, 128 * k:128 * k + 128]) for k in range(8)]
    for g in range(8):
        row = rep_f[:, 128 * g:128 * g + 128]
        acc = jnp.zeros((128, 128), F32)
        for k in range(8):
            acc = acc + jnp.where(cols_f[k] < row, 1.0, 0.0)
        counts.append(jnp.sum(acc, axis=0, keepdims=True))
    rank = jnp.concatenate(counts, axis=1)
    rank_i = rank.astype(jnp.int32)
    blk_i = rep_i >> 10
    bx, bz, bc = blk_i >> 3, (blk_i >> 1) & 3, blk_i & 1
    slot = jnp.where(bc == 0, bz * 4 + bx, 16 + bx * 4 + bz)
    prow = (32 * slot + rank_i - 32 * blk_i).astype(F32)

    mine = (lax.axis_index("scen")).astype(F32)
    jot = lax.broadcasted_iota(jnp.int32, (32, ROWS), 0).astype(F32)
    hit = (rank - 32.0 * mine) == jot
    pos = jnp.sum(jnp.where(hit, rep_f, 0.0), axis=1, keepdims=True) - 1024.0 * mine
    sel = jnp.where(
        lax.broadcasted_iota(jnp.int32, (32, ROWS), 1).astype(F32) == pos, 1.0, 0.0
    ).astype(BF)

    def blk(name, cc, lo=0, hi=EXT):
        t, k = SPOT[name]
        return reps_v.at[t, cc, pl.ds(32 * k, 32), pl.ds(lo, hi - lo)]

    def go(src, dst, ssem, rsem, to):
        remote(src, dst, ssem, rsem, to).start()

    def recv(buf, rsem):
        remote(buf, buf, f_send.at[0], rsem, partner).wait_recv()

    def sent(buf, ssem):
        remote(buf, buf, ssem, f_recv.at[0], partner).wait_send()

    def first(i, name, there, h, to):
        go(blk(name, c, *QUARTERS[h]), blk(there, c, *QUARTERS[h]), f_send.at[0], f_recv.at[i], to)

    def first_wait(i, name, lo, hi):
        recv(blk(name, c, lo, hi), f_recv.at[i])

    total = jnp.zeros((32, 1), F32)
    for k in range(4):
        loads[k].wait()
        cols = slice(k * 1024, (k + 1) * 1024)
        own = jnp.dot(sel, scen_v[:, cols], preferred_element_type=F32)
        reps_v[0, c, 0:32, cols] = own.astype(BF)
        total = total + jnp.sum(own * own, axis=1, keepdims=True)
        if k == 0:
            meet(7)
        if k < 3:
            first(min(k, 2), "O0", "O3", k, f_up)
            first(3 if k < 2 else 2 + k, "O0", "O1", k, f_dn)
    hi, mid, low = split3(total)
    lane = lax.broadcasted_iota(jnp.int32, (32, 128), 1)
    ext = jnp.where(lane == 0, hi.astype(F32),
                    jnp.where(lane == 1, mid.astype(F32),
                              jnp.where(lane == 2, low.astype(F32), 0.0)))
    reps_v[0, c, 0:32, FY:EXT] = ext.astype(BF)
    first(2, "O0", "O3", 3, f_up)
    first(5, "O0", "O1", 3, f_dn)

    def to_partner(name):
        t, _ = SPOT[name]
        go(blk(name, c), blk(name, c), c_send.at[t], c_recv.at[t], partner)

    def from_partner(t):
        recv(reps_v.at[t, 1 - c], c_recv.at[t])

    def second(r, up):
        i, there, to = (0, "U%d" % r, s_up) if up else (1, "D%d" % r, s_dn)
        go(blk("O%d" % r, c), blk(there, c), s_send.at[0], s_recv.at[i, r], to)

    def arrive(name):
        group, r = name[0], int(name[1])
        recv(blk(name, c), s_recv.at["UDF".index(group), r])
        if name in ("U0", "U3", "D1", "D2"):
            go(blk(name, c), blk("F%d" % r, c), s_send.at[0], s_recv.at[2, r],
               s_up if group == "U" else s_dn)
        to_partner(name)

    second(0, True)
    second(0, False)
    to_partner("O0")

    def norms(i, _):
        rows = pl.ds(pl.multiple_of(i * 128, 128), 128)
        acc = jnp.zeros((128, 128), F32)
        for k in range(32):
            v = scen_v[rows, k * 128:(k + 1) * 128].astype(F32)
            acc = acc + v * v
        wide = jnp.broadcast_to(jnp.sum(acc, axis=1, keepdims=True), (128, 128))
        sqs[i] = jnp.transpose(wide)[0:8, :]
        return 0

    def permutation():
        for k in range(8):
            col = column(prow[:, 128 * k:128 * k + 128])
            for g in range(8):
                lane = lax.broadcasted_iota(jnp.int32, (128, 128), 1).astype(F32) + 128.0 * g
                pi[128 * k:128 * k + 128, 128 * g:128 * g + 128] = jnp.where(
                    col == lane, 1.0, 0.0).astype(BF)

    for h in range(2):
        first_wait(h, "O3", *QUARTERS[h])
        first(6, "O3", "O2", h, f_up)
    first_wait(3, "O1", 0, 2048)
    for h in range(2, 4):
        first_wait(2 + h, "O1", *QUARTERS[h])
        first(6, "O1", "O2", h, f_dn)
    second(1, False)
    to_partner("O1")
    first_wait(2, "O3", 2048, EXT)
    second(3, True)
    to_partner("O3")
    arrive("U0")
    second(1, True)
    second(3, False)

    ones8 = jnp.ones((8, 128), BF)
    firsts, seconds = (ya, yb), (yb, ya)

    def send1(t, h, k):
        return remote(snd1.at[t, k, h], rcv1.at[t, k, h], r1_send.at[0], r1_recv.at[t, k],
                      at_y(firsts[h]))

    def matmul(t, after=()):
        ext = reps_v[t, :, :, FY:EXT].reshape(256, 128)
        sqr = lax.dot_general(ones8, ext, NT, preferred_element_type=F32)
        for h in range(2):
            sq_buf[y, 2 * t + h] = sqr[:, 128 * h:128 * h + 128]
        if t == 3:
            for k in (1, 0, 2):
                go(sq_buf.at[y], sq_buf.at[y], q_send.at[0], q_recv.at[0], ring[k])

        def tile(m, _):
            d = jnp.where(m == 0, yc, jnp.where(m == 1, ya, jnp.where(m == 2, yb, y)))
            cross = lax.dot_general(
                scen_v[pl.ds(pl.multiple_of(d * 256, 256), 256), :],
                reps_v[t, :, :, 0:FY].reshape(256, FY), NT, preferred_element_type=F32)
            lo, hi = cross[:, :128], cross[:, 128:]
            part[t, 0, m] = lo
            part[t, 1, m] = hi

            @pl.when(m == 0)
            def _():
                snd1[t, 1, 0] = pack(lo, SCALE1)
                send1(t, 0, 1).start()
                snd1[t, 1, 1] = pack(hi, SCALE1)
                send1(t, 1, 1).start()

            @pl.when(m == 1)
            def _():
                snd1[t, 0, 0] = pack(lo, SCALE1)
                send1(t, 0, 0).start()

            @pl.when(m == 2)
            def _():
                snd1[t, 0, 1] = pack(hi, SCALE1)
                send1(t, 1, 0).start()

            for k, act in enumerate(after):
                pl.when(m == k)(act)
            return 0

        lax.fori_loop(0, 4, tile, 0)

    def reduce2(t):
        recv(rcv1.at[t, 1], r1_recv.at[t, 1])
        for h in range(2):
            snd2[t, h] = pack(part[t, h, 2 - h] + unpack(rcv1[t, 1, h], SCALE1), SCALE2)
            go(snd2.at[t, h], rcv2.at[t, h], r2_send.at[0], r2_recv.at[t], at_y(seconds[h]))

    def finish(t, h):
        if h == 0:
            recv(rcv1.at[t, 0], r1_recv.at[t, 0])
            recv(rcv2.at[t], r2_recv.at[t])
        whole = part[t, h, 3] + unpack(rcv1[t, 0, h], SCALE1) + unpack(rcv2[t, h], SCALE2)
        g = 2 * t + h
        sq_r = sq_buf[0, g] + sq_buf[1, g] + sq_buf[2, g] + sq_buf[3, g]
        return ((sq_s + sq_r[0:1, :]) - 2.0 * whole) * (1.0 / (F * EPS))

    def settle(h, d, value):
        if h == 0:
            cost[(z + d) % 4] = pltpu.roll(value, 32 * x, 1)
        else:
            cost[4 + (x + d) % 4] = pltpu.roll(value, 32 * z, 1)

    def far_along():
        first_wait(6, "O2", 0, EXT)
        second(2, False)
        to_partner("O2")

    def acts(*names):
        def act():
            for name in names:
                far_along() if name == "O2" else arrive(name)
        return act

    lax.fori_loop(0, 4, norms, 0)
    from_partner(0)
    matmul(0, (acts("D0"), acts("O2"), acts(), acts("D1")))
    arrive("U3")
    second(2, True)
    lax.fori_loop(4, 8, norms, 0)
    reduce2(0)
    from_partner(1)
    sq_buf[y, 8] = jnp.concatenate([sqs[k, 0:1, :] for k in range(8)], axis=0)
    matmul(1, (acts(), acts("F0"), acts("D3"), acts("U1")))
    arrive("D2")
    from_partner(2)
    matmul(2, (acts(), lambda: reduce2(1), acts("F1"), acts("F3")))
    arrive("U2")
    arrive("F2")
    permutation()
    from_partner(3)
    matmul(3, (lambda: None, lambda: reduce2(2)))
    reduce2(3)
    recv(sq_buf.at[0:3], q_recv.at[0])
    sqs[0] = sq_buf[0, 8] + sq_buf[1, 8] + sq_buf[2, 8] + sq_buf[3, 8]
    sq_s = jnp.concatenate(
        [column(sqs[0, pl.ds(2 * y + k, 1), :]) for k in range(2)], axis=0)
    place_of = lax.broadcasted_iota(jnp.int32, (256, 128), 1) // 32
    for t in range(3):
        for h in range(2):
            keep[t, h] = finish(t, h)
            if t == 1:
                settle(h, 0, jnp.where(place_of == 2, keep[1, h], keep[0, h]))
        if t == 2:
            for h in range(2):
                settle(h, 1, jnp.where(place_of < 2, keep[1, h], keep[2, h]))
    for h in range(2):
        last = finish(3, h)
        settle(h, 3, jnp.where(place_of == 0, pltpu.roll(keep[0, h], 64, 1),
                               jnp.where(place_of == 1, keep[2, h],
                                         jnp.where(place_of == 2, pltpu.roll(last, 64, 1),
                                                   keep[1, h]))))
        settle(h, 2, jnp.where(place_of == 0, keep[2, h], last))

    def rows_of(q):
        return pi[pl.ds(pl.multiple_of(q * 256, 256), 256), :]

    def col_of(q):
        return pl.ds(pl.multiple_of(q * 256, 256), 256)

    here = col_of(y)

    def permuted(q):
        out = None
        for k in range(3):
            some = lax.dot_general(rows_of(q), split[k], NT, preferred_element_type=F32)
            out = some if out is None else out + some
        return out

    def make_split():
        for g in range(8):
            for k, piece in enumerate(split3(cost[g])):
                split[k, :, 128 * g:128 * g + 128] = piece

    up, dn = ring[0], ring[2]
    cuts = ((0, 96), (96, 96), (192, 64))

    def row_piece(n):
        rows = pl.ds(*cuts[n])
        for k, to in ((0, up), (1, dn)):
            go(row_snd.at[k, rows], row_cost.at[rows, here], sm.at[0], rm.at[3], to)

    v = jnp.zeros((8, 128), F32)
    for it in range(ITERS):
        peak = None
        for g in range(8):
            s = v[g:g + 1, :] - cost[g]
            peak = s if peak is None else jnp.maximum(peak, s)
        peak = jnp.max(peak, axis=1, keepdims=True)
        acc = None
        for g in range(8):
            e = jnp.exp((v[g:g + 1, :] - cost[g]) - peak)
            acc = e if acc is None else acc + e
        u = -math.log(COUNT_S) - (peak + jnp.log(jnp.sum(acc, axis=1, keepdims=True)))
        rows = []
        for g in range(8):
            s = u - cost[g]
            top = jnp.max(s, axis=0, keepdims=True)
            rows.append(top + jnp.log(jnp.sum(jnp.exp(s - top), axis=0, keepdims=True)))
        box1[it] = jnp.concatenate(rows, axis=0)
        for k in NEAR_ORDER:
            go(box1.at[it], in1.at[it, me1], s1.at[it], r1.at[it], near[k])
        in1[it, me1] = box1[it]
        if it == 0:
            make_split()
            row_snd[2] = permuted(yc)
            row_snd[0] = permuted((y + 1) % 4)
        if it == ITERS - 1:
            wide = jnp.broadcast_to(u, (256, 128))
            flat = [jnp.transpose(wide[128 * k:128 * k + 128, :])[0:1, :] for k in range(2)]
            u_buf[4] = jnp.concatenate(flat + [jnp.zeros((6, 128), F32)], axis=0)
            u_buf[y] = u_buf[4]
            for k in range(3):
                go(u_buf.at[4], u_buf.at[y], su.at[0], ru.at[0], ring[k])
        recv(in1.at[it, 0:7], r1.at[it])
        box2[it] = lse([in1[it, k] for k in range(8)])
        for k in FAR_ORDER:
            go(box2.at[it], in2.at[it, plane], s2.at[it], r2.at[it], far[k])
        in2[it, plane] = box2[it]
        if it == 0:
            go(row_snd.at[2, 0:128], relay.at[0], sm.at[0], rm.at[0], up)
            go(row_snd.at[2, 128:256], relay.at[1], sm.at[0], rm.at[1], dn)
            row_snd[1] = permuted((y + 3) % 4)
            row_piece(0)
            row_snd[3] = permuted(y)
            kept = pltpu.make_async_copy(row_snd.at[3], row_cost.at[:, here], hbm_sem.at[4])
            kept.start()
        if it == 1:
            recv(relay.at[0], rm.at[0])
            go(relay.at[0], row_cost.at[0:128, col_of((y + 3) % 4)], sm.at[0], rm.at[2], up)
            recv(relay.at[1], rm.at[1])
            go(relay.at[1], row_cost.at[128:256, col_of((y + 1) % 4)], sm.at[0], rm.at[2], dn)
            row_piece(1)
        if it == ITERS - 1:
            recv(u_buf.at[0:3], ru.at[0])
            row_piece(2)
            recv(row_cost.at[:, col_of(yc)], rm.at[2])
            kept.wait()
            u_out[...] = jnp.concatenate([u_buf[k, 0:2, :] for k in range(4)], axis=0)
            u_copy = pltpu.make_async_copy(u_out, u_ref, hbm_sem.at[0])
            u_copy.start()
            sent(reps_v.at[0, c, 0:96], f_send.at[0])
            sent(reps_v.at[0:3, c], s_send.at[0])
            for t in range(4):
                sent(reps_v.at[t, c], c_send.at[t])
            sent(snd1, r1_send.at[0])
            sent(snd2, r2_send.at[0])
            sent(sq_buf.at[0:3], q_send.at[0])
        recv(in2.at[it, 0:15], r2.at[it])
        sent(in1.at[it, 0:7], s1.at[it])
        sent(in2.at[it, 0:15], s2.at[it])
        v = -math.log(COUNT_R) - lse([in2[it, k] for k in range(16)])

    flat = jnp.concatenate([v[g:g + 1, :] for g in range(8)], axis=1)
    pieces = split3(flat)
    row = lax.broadcasted_iota(jnp.int32, (8, 1024), 0)
    three = jnp.where(row == 0, pieces[0].astype(F32),
                      jnp.where(row == 1, pieces[1].astype(F32),
                                jnp.where(row == 2, pieces[2].astype(F32), 0.0))).astype(BF)
    got = lax.dot_general(three, rows_of(y), NT, preferred_element_type=F32)
    v_out[...] = got[0:1, :] + got[1:2, :] + got[2:3, :]
    v_copy = pltpu.make_async_copy(v_out, v_ref, hbm_sem.at[1])
    v_copy.start()
    recv(row_cost.at[:, 0:512], rm.at[3])
    sent(row_snd, sm.at[0])
    sent(u_buf.at[0:3], su.at[0])
    u_copy.wait()
    v_copy.wait()


VM = pl.BlockSpec(memory_space=pltpu.VMEM)
ANY = pl.BlockSpec(memory_space=pl.ANY)


def emit(u_ref, v_ref, cost_ref, u_out, v_out, mem_out, u_buf, v_buf, m_buf, sem):
    u_buf[...] = u_ref[...] * EPS
    v_buf[...] = v_ref[...] * EPS
    copies = [pltpu.make_async_copy(u_buf, u_out, sem.at[0]),
              pltpu.make_async_copy(v_buf, v_out, sem.at[1])]
    for cp in copies:
        cp.start()
    for h in range(2):
        half = slice(128 * h, 128 * h + 128)
        v_col = column(v_ref[:, half])
        for k in range(8):
            cols = slice(128 * k, 128 * k + 128)
            m_buf[half, cols] = (
                COUNT_S * jnp.exp((u_ref[k:k + 1, :] + v_col) - cost_ref[half, cols])).astype(BF)
        cp = pltpu.make_async_copy(m_buf.at[half], mem_out.at[half], sem.at[2 + h])
        cp.start()
        copies.append(cp)
    for cp in copies:
        cp.wait()


def on_device(scenarios, rep_index):
    dma = pltpu.SemaphoreType.DMA
    shapes = (jax.ShapeDtypeStruct((8, 128), F32),
              jax.ShapeDtypeStruct((1, 256), F32),
              jax.ShapeDtypeStruct((256, 1024), BF))
    results = pl.pallas_call(
        kernel,
        out_shape=shapes[:2] + (jax.ShapeDtypeStruct((256, 1024), F32),),
        in_specs=[pl.BlockSpec(memory_space=pltpu.HBM)] * 2,
        out_specs=(ANY, ANY, ANY),
        scratch_shapes=[
            pltpu.VMEM((ROWS, FY), BF),
            pltpu.VMEM((4, 2, 128, EXT), BF),
            pltpu.VMEM((4, 2, 4, 256, 128), F32),
            pltpu.VMEM((4, 2, 2, 192, 128), jnp.int32),
            pltpu.VMEM((4, 2, 2, 192, 128), jnp.int32),
            pltpu.VMEM((4, 2, 192, 128), jnp.int32),
            pltpu.VMEM((4, 2, 192, 128), jnp.int32),
            pltpu.VMEM((8, 8, 128), F32),
            pltpu.VMEM((8, 256, 128), F32),
            pltpu.VMEM((1, 1024), jnp.int32),
            pltpu.VMEM((1024, 1024), BF),
            pltpu.VMEM((4, 9, 8, 128), F32),
            pltpu.VMEM((5, 8, 128), F32),
            pltpu.VMEM((3, 8, 8, 128), F32),
            pltpu.VMEM((3, 16, 8, 128), F32),
            pltpu.VMEM((3, 8, 128), F32),
            pltpu.VMEM((3, 8, 128), F32),
            pltpu.VMEM((3, 2, 256, 128), F32),
            pltpu.VMEM((3, 256, 1024), BF),
            pltpu.VMEM((4, 256, 256), F32),
            pltpu.VMEM((2, 128, 256), F32),
            pltpu.VMEM((8, 128), F32),
            pltpu.VMEM((1, 256), F32),
            dma((5,)), dma((1,)), dma((7,)), dma((1,)), dma((3, 4)), dma((4,)), dma((4,)),
            dma((1,)), dma((4, 2)), dma((1,)), dma((4,)), dma((1,)), dma((1,)),
            dma((3,)), dma((3,)), dma((3,)), dma((3,)), dma((1,)), dma((1,)),
            dma((1,)), dma((4,)),
        ],
        compiler_params=pltpu.CompilerParams(
            collective_id=0, has_side_effects=True, vmem_limit_bytes=50 << 20),
        name="transport",
    )(pltpu.with_memory_space_constraint(rep_index.reshape(1, 1024), pltpu.HBM), scenarios)
    u, v, member = pl.pallas_call(
        emit,
        out_shape=shapes,
        in_specs=[VM] * 3,
        out_specs=(ANY, ANY, ANY),
        scratch_shapes=[pltpu.VMEM((8, 128), F32), pltpu.VMEM((1, 256), F32),
                        pltpu.VMEM((256, 1024), BF), dma((4,))],
        compiler_params=pltpu.CompilerParams(vmem_limit_bytes=4 << 20),
        name="emit",
    )(*results)
    return u.reshape(1024), v.reshape(256), member


def solution(mesh):
    return jax.shard_map(
        on_device,
        mesh=mesh,
        in_specs=(P("scen", "rep"), P()),
        out_specs=(P("scen"), P("rep"), P("rep", "scen")),
        check_vma=False,
    )
```

```python
import functools
import math

import jax
import jax.numpy as jnp
from jax import lax
from jax.experimental import pallas as pl
from jax.experimental.pallas import tpu as pltpu
from jax.sharding import PartitionSpec as P

F = 16384
ITERS = 3
COUNT_S = 32768
COUNT_R = 1024
EPS = 0.1
FY = 4096
ROWS = 1024
EXT = FY + 128
QUARTERS = ((0, 1024), (1024, 2048), (2048, 3072), (3072, EXT))
MESH = pl.DeviceIdType.MESH
BF = jnp.bfloat16
F32 = jnp.float32
NT = (((1,), (1,)), ((), ()))


def remote(src, dst, ssem, rsem, dev):
    return pltpu.make_async_remote_copy(
        src_ref=src, dst_ref=dst, send_sem=ssem, recv_sem=rsem, device_id=dev, device_id_type=MESH
    )


def place():
    scen = lax.axis_index("scen")
    y = lax.axis_index("rep")
    return scen // 8, (scen // 2) % 4, scen % 2, y


def dev(x, z, c, y):
    return ((x * 4 + z) * 2 + c, y)


def greet(peers):
    sem = pltpu.get_barrier_semaphore()
    for p in peers:
        pl.semaphore_signal(sem, inc=1, device_id=p, device_id_type=MESH)


def meet(count):
    pl.semaphore_wait(pltpu.get_barrier_semaphore(), count)


def column(row):
    return jnp.transpose(jnp.broadcast_to(row, (128, 128)))


def split3(v):
    hi = v.astype(BF)
    rest = v - hi.astype(F32)
    mid = rest.astype(BF)
    low = (rest - mid.astype(F32)).astype(BF)
    return hi, mid, low


TOP = 2 ** 20 - 1


def pack(x):
    k = jnp.floor(jnp.max(jnp.abs(x), axis=0, keepdims=True) * 0.125) + 1.0
    q = jnp.round(x * ((TOP / 8.0) / k)).astype(jnp.int32)
    third = jnp.concatenate(
        [q[176:], jnp.broadcast_to(k, (8, 128)).astype(jnp.int32)], axis=0)
    return jnp.concatenate(
        [(q[:88] << 11) | (third & 2047), (q[88:176] << 11) | ((third >> 11) & 1023)], axis=0)


def unpack(w):
    one, two = w[:88], w[88:]
    third = ((two << 22) >> 11) | (one & 2047)
    step = third[80:81].astype(F32) * (8.0 / TOP)
    return jnp.concatenate([one >> 11, two >> 11, third[:80]], axis=0).astype(F32) * step


SPOT = {
    "O0": (0, 0), "O1": (0, 1), "U0": (0, 2), "O3": (0, 3),
    "D0": (1, 0), "D1": (1, 1), "O2": (1, 2), "U3": (1, 3),
    "F0": (2, 0), "U1": (2, 1), "D2": (2, 2), "D3": (2, 3),
    "U2": (3, 0), "F1": (3, 1), "F2": (3, 2), "F3": (3, 3),
}
NEAR_ORDER = (3, 4, 2, 5, 1, 6, 0)
FAR_ORDER = tuple(sorted(range(15), key=lambda k: -(min((k + 1) % 4, 4 - (k + 1) % 4)
                                                   + min((k + 1) // 4, 4 - (k + 1) // 4))))


def lse(rows):
    peak = functools.reduce(jnp.maximum, rows)
    return peak + jnp.log(functools.reduce(jnp.add, [jnp.exp(r - peak) for r in rows]))


def kernel(rep_hbm, scen_hbm, u_ref, v_ref, row_cost,
           scen_v, reps_v, part, snd1, rcv1, snd2, rcv2, sqs, cost, rep_v, pi, sq_buf,
           u_buf, in1, in2, box1, box2, keep, split, row_snd, relay, u_out, v_out,
           hbm_sem, f_send, f_recv, s_send, s_recv, c_send, c_recv, r1_send, r1_recv,
           r2_send, r2_recv, q_send, q_recv, s1, r1, s2, r2, su, ru, sm, rm):
    x, z, c, y = place()
    pf = x * (1 - c) + z * c
    ps = z * (1 - c) + x * c

    def along_first(d):
        return dev((x + (1 - c) * d) % 4, (z + c * d) % 4, c, y)

    def along_second(d):
        return dev((x + c * d) % 4, (z + (1 - c) * d) % 4, c, y)

    f_up, f_dn = along_first(1), along_first(3)
    s_up, s_dn = along_second(1), along_second(3)
    partner = dev(x, z, 1 - c, y)
    ya = y + 1 - 2 * (y % 2)
    yb = 3 - y
    yc = (y + 2) % 4
    at_y = lambda q: dev(x, z, c, q)
    plane = x * 4 + z
    me1 = y * 2 + c
    near, far = [], []
    for k in range(1, 8):
        q = (me1 + k) % 8
        near.append(dev(x, z, q % 2, q // 2))
    for k in range(1, 16):
        q = (plane + k) % 16
        far.append(dev(q // 4, q % 4, c, y))
    ring = [at_y((y + k) % 4) for k in range(1, 4)]

    rep_load = pltpu.make_async_copy(rep_hbm, rep_v, hbm_sem.at[4])
    rep_load.start()
    loads = []
    for k in range(4):
        cols = pl.ds(k * 1024, 1024)
        cp = pltpu.make_async_copy(scen_hbm.at[:, cols], scen_v.at[:, cols], hbm_sem.at[k])
        cp.start()
        loads.append(cp)
    greet([f_up, f_dn, s_up, s_dn, partner, at_y(ya), at_y(yb)])
    rep_load.wait()

    rep_i = rep_v[...]
    rep_f = rep_i.astype(F32)
    counts = []
    cols_f = [column(rep_f[:, 128 * k:128 * k + 128]) for k in range(8)]
    for g in range(8):
        row = rep_f[:, 128 * g:128 * g + 128]
        acc = jnp.zeros((128, 128), F32)
        for k in range(8):
            acc = acc + jnp.where(cols_f[k] < row, 1.0, 0.0)
        counts.append(jnp.sum(acc, axis=0, keepdims=True))
    rank = jnp.concatenate(counts, axis=1)
    rank_i = rank.astype(jnp.int32)
    blk_i = rep_i >> 10
    bx, bz, bc = blk_i >> 3, (blk_i >> 1) & 3, blk_i & 1
    slot = jnp.where(bc == 0, bz * 4 + bx, 16 + bx * 4 + bz)
    prow = (32 * slot + rank_i - 32 * blk_i).astype(F32)

    mine = (lax.axis_index("scen")).astype(F32)
    jot = lax.broadcasted_iota(jnp.int32, (32, ROWS), 0).astype(F32)
    hit = (rank - 32.0 * mine) == jot
    pos = jnp.sum(jnp.where(hit, rep_f, 0.0), axis=1, keepdims=True) - 1024.0 * mine
    sel = jnp.where(
        lax.broadcasted_iota(jnp.int32, (32, ROWS), 1).astype(F32) == pos, 1.0, 0.0
    ).astype(BF)

    def blk(name, cc, lo=0, hi=EXT):
        t, k = SPOT[name]
        return reps_v.at[t, cc, pl.ds(32 * k, 32), pl.ds(lo, hi - lo)]

    def go(src, dst, ssem, rsem, to):
        remote(src, dst, ssem, rsem, to).start()

    def recv(buf, rsem):
        remote(buf, buf, f_send.at[0], rsem, partner).wait_recv()

    def sent(buf, ssem):
        remote(buf, buf, ssem, f_recv.at[0], partner).wait_send()

    def first(i, name, there, h, to):
        go(blk(name, c, *QUARTERS[h]), blk(there, c, *QUARTERS[h]), f_send.at[0], f_recv.at[i], to)

    def first_wait(i, name, lo, hi):
        recv(blk(name, c, lo, hi), f_recv.at[i])

    total = jnp.zeros((32, 1), F32)
    for k in range(4):
        loads[k].wait()
        cols = slice(k * 1024, (k + 1) * 1024)
        own = jnp.dot(sel, scen_v[:, cols], preferred_element_type=F32)
        reps_v[0, c, 0:32, cols] = own.astype(BF)
        total = total + jnp.sum(own * own, axis=1, keepdims=True)
        if k == 0:
            meet(7)
        if k < 3:
            first(min(k, 2), "O0", "O3", k, f_up)
            first(3 if k < 2 else 2 + k, "O0", "O1", k, f_dn)
    hi, mid, low = split3(total)
    lane = lax.broadcasted_iota(jnp.int32, (32, 128), 1)
    ext = jnp.where(lane == 0, hi.astype(F32),
                    jnp.where(lane == 1, mid.astype(F32),
                              jnp.where(lane == 2, low.astype(F32), 0.0)))
    reps_v[0, c, 0:32, FY:EXT] = ext.astype(BF)
    first(2, "O0", "O3", 3, f_up)
    first(5, "O0", "O1", 3, f_dn)

    def to_partner(name):
        t, _ = SPOT[name]
        go(blk(name, c), blk(name, c), c_send.at[t], c_recv.at[t], partner)

    def from_partner(t):
        recv(reps_v.at[t, 1 - c], c_recv.at[t])

    def second(r, up):
        i, there, to = (0, "U%d" % r, s_up) if up else (1, "D%d" % r, s_dn)
        go(blk("O%d" % r, c), blk(there, c), s_send.at[0], s_recv.at[i, r], to)

    def arrive(name):
        group, r = name[0], int(name[1])
        recv(blk(name, c), s_recv.at["UDF".index(group), r])
        if name in ("U0", "U3", "D1", "D2"):
            go(blk(name, c), blk("F%d" % r, c), s_send.at[0], s_recv.at[2, r],
               s_up if group == "U" else s_dn)
        to_partner(name)

    second(0, True)
    second(0, False)
    to_partner("O0")

    def norms(i, _):
        rows = pl.ds(pl.multiple_of(i * 128, 128), 128)
        acc = jnp.zeros((128, 128), F32)
        for k in range(32):
            v = scen_v[rows, k * 128:(k + 1) * 128].astype(F32)
            acc = acc + v * v
        wide = jnp.broadcast_to(jnp.sum(acc, axis=1, keepdims=True), (128, 128))
        sqs[i] = jnp.transpose(wide)[0:8, :]
        return 0

    def permutation():
        for k in range(8):
            col = column(prow[:, 128 * k:128 * k + 128])
            for g in range(8):
                lane = lax.broadcasted_iota(jnp.int32, (128, 128), 1).astype(F32) + 128.0 * g
                pi[128 * k:128 * k + 128, 128 * g:128 * g + 128] = jnp.where(
                    col == lane, 1.0, 0.0).astype(BF)

    for h in range(2):
        first_wait(h, "O3", *QUARTERS[h])
        first(6, "O3", "O2", h, f_up)
    first_wait(3, "O1", 0, 2048)
    for h in range(2, 4):
        first_wait(2 + h, "O1", *QUARTERS[h])
        first(6, "O1", "O2", h, f_dn)
    second(1, False)
    to_partner("O1")
    first_wait(2, "O3", 2048, EXT)
    second(3, True)
    to_partner("O3")
    arrive("U0")
    second(1, True)
    second(3, False)

    ones8 = jnp.ones((8, 128), BF)
    firsts, seconds = (ya, yb), (yb, ya)

    def send1(t, h, k):
        return remote(snd1.at[t, k, h], rcv1.at[t, k, h], r1_send.at[0], r1_recv.at[t, k],
                      at_y(firsts[h]))

    def matmul(t, after=()):
        ext = reps_v[t, :, :, FY:EXT].reshape(256, 128)
        sqr = lax.dot_general(ones8, ext, NT, preferred_element_type=F32)
        for h in range(2):
            sq_buf[y, 2 * t + h] = sqr[:, 128 * h:128 * h + 128]
        if t == 3:
            for k in (1, 0, 2):
                go(sq_buf.at[y], sq_buf.at[y], q_send.at[0], q_recv.at[0], ring[k])

        def tile(m, _):
            d = jnp.where(m == 0, yc, jnp.where(m == 1, ya, jnp.where(m == 2, yb, y)))
            cross = lax.dot_general(
                scen_v[pl.ds(pl.multiple_of(d * 256, 256), 256), :],
                reps_v[t, :, :, 0:FY].reshape(256, FY), NT, preferred_element_type=F32)
            lo, hi = cross[:, :128], cross[:, 128:]
            part[t, 0, m] = lo
            part[t, 1, m] = hi

            @pl.when(m == 0)
            def _():
                snd1[t, 1, 0] = pack(lo)
                send1(t, 0, 1).start()
                snd1[t, 1, 1] = pack(hi)
                send1(t, 1, 1).start()

            @pl.when(m == 1)
            def _():
                snd1[t, 0, 0] = pack(lo)
                send1(t, 0, 0).start()

            @pl.when(m == 2)
            def _():
                snd1[t, 0, 1] = pack(hi)
                send1(t, 1, 0).start()

            for k, act in enumerate(after):
                pl.when(m == k)(act)
            return 0

        lax.fori_loop(0, 4, tile, 0)

    def reduce2(t):
        recv(rcv1.at[t, 1], r1_recv.at[t, 1])
        for h in range(2):
            snd2[t, h] = pack(part[t, h, 2 - h] + unpack(rcv1[t, 1, h]))
            go(snd2.at[t, h], rcv2.at[t, h], r2_send.at[0], r2_recv.at[t], at_y(seconds[h]))

    def finish(t, h):
        if h == 0:
            recv(rcv1.at[t, 0], r1_recv.at[t, 0])
            recv(rcv2.at[t], r2_recv.at[t])
        whole = part[t, h, 3] + unpack(rcv1[t, 0, h]) + unpack(rcv2[t, h])
        g = 2 * t + h
        sq_r = sq_buf[0, g] + sq_buf[1, g] + sq_buf[2, g] + sq_buf[3, g]
        return ((sq_s + sq_r[0:1, :]) - 2.0 * whole) * (1.0 / (F * EPS))

    def settle(h, d, value):
        if h == 0:
            cost[(z + d) % 4] = pltpu.roll(value, 32 * x, 1)
        else:
            cost[4 + (x + d) % 4] = pltpu.roll(value, 32 * z, 1)

    def far_along():
        first_wait(6, "O2", 0, EXT)
        second(2, False)
        to_partner("O2")

    def acts(*names):
        def act():
            for name in names:
                far_along() if name == "O2" else arrive(name)
        return act

    lax.fori_loop(0, 4, norms, 0)
    from_partner(0)
    matmul(0, (acts("D0"), acts("O2"), acts(), acts("D1")))
    arrive("U3")
    second(2, True)
    lax.fori_loop(4, 8, norms, 0)
    reduce2(0)
    from_partner(1)
    sq_buf[y, 8] = jnp.concatenate([sqs[k, 0:1, :] for k in range(8)], axis=0)
    matmul(1, (acts(), acts("F0"), acts("D3"), acts("U1")))
    arrive("D2")
    from_partner(2)
    matmul(2, (acts(), lambda: reduce2(1), acts("F1"), acts("F3")))
    arrive("U2")
    arrive("F2")
    permutation()
    from_partner(3)
    matmul(3, (lambda: None, lambda: reduce2(2)))
    reduce2(3)
    recv(sq_buf.at[0:3], q_recv.at[0])
    sqs[0] = sq_buf[0, 8] + sq_buf[1, 8] + sq_buf[2, 8] + sq_buf[3, 8]
    sq_s = jnp.concatenate(
        [column(sqs[0, pl.ds(2 * y + k, 1), :]) for k in range(2)], axis=0)
    place_of = lax.broadcasted_iota(jnp.int32, (256, 128), 1) // 32
    for t in range(3):
        for h in range(2):
            keep[t, h] = finish(t, h)
            if t == 1:
                settle(h, 0, jnp.where(place_of == 2, keep[1, h], keep[0, h]))
        if t == 2:
            for h in range(2):
                settle(h, 1, jnp.where(place_of < 2, keep[1, h], keep[2, h]))
    for h in range(2):
        last = finish(3, h)
        settle(h, 3, jnp.where(place_of == 0, pltpu.roll(keep[0, h], 64, 1),
                               jnp.where(place_of == 1, keep[2, h],
                                         jnp.where(place_of == 2, pltpu.roll(last, 64, 1),
                                                   keep[1, h]))))
        settle(h, 2, jnp.where(place_of == 0, keep[2, h], last))

    def rows_of(q):
        return pi[pl.ds(pl.multiple_of(q * 256, 256), 256), :]

    def col_of(q):
        return pl.ds(pl.multiple_of(q * 256, 256), 256)

    here = col_of(y)

    def permuted(q):
        out = None
        for k in range(3):
            some = lax.dot_general(rows_of(q), split[k], NT, preferred_element_type=F32)
            out = some if out is None else out + some
        return out

    def make_split():
        for g in range(8):
            for k, piece in enumerate(split3(cost[g])):
                split[k, :, 128 * g:128 * g + 128] = piece

    up, dn = ring[0], ring[2]
    cuts = ((0, 96), (96, 96), (192, 64))

    def row_piece(n):
        rows = pl.ds(*cuts[n])
        for k, to in ((0, up), (1, dn)):
            go(row_snd.at[k, rows], row_cost.at[rows, here], sm.at[0], rm.at[3], to)

    v = jnp.zeros((8, 128), F32)
    for it in range(ITERS):
        peak = None
        for g in range(8):
            s = v[g:g + 1, :] - cost[g]
            peak = s if peak is None else jnp.maximum(peak, s)
        peak = jnp.max(peak, axis=1, keepdims=True)
        acc = None
        for g in range(8):
            e = jnp.exp((v[g:g + 1, :] - cost[g]) - peak)
            acc = e if acc is None else acc + e
        u = -math.log(COUNT_S) - (peak + jnp.log(jnp.sum(acc, axis=1, keepdims=True)))
        rows = []
        for g in range(8):
            s = u - cost[g]
            top = jnp.max(s, axis=0, keepdims=True)
            rows.append(top + jnp.log(jnp.sum(jnp.exp(s - top), axis=0, keepdims=True)))
        box1[it] = jnp.concatenate(rows, axis=0)
        for k in NEAR_ORDER:
            go(box1.at[it], in1.at[it, me1], s1.at[it], r1.at[it], near[k])
        in1[it, me1] = box1[it]
        if it == 0:
            make_split()
            row_snd[2] = permuted(yc)
            row_snd[0] = permuted((y + 1) % 4)
        if it == ITERS - 1:
            wide = jnp.broadcast_to(u, (256, 128))
            flat = [jnp.transpose(wide[128 * k:128 * k + 128, :])[0:1, :] for k in range(2)]
            u_buf[4] = jnp.concatenate(flat + [jnp.zeros((6, 128), F32)], axis=0)
            u_buf[y] = u_buf[4]
            for k in range(3):
                go(u_buf.at[4], u_buf.at[y], su.at[0], ru.at[0], ring[k])
        recv(in1.at[it, 0:7], r1.at[it])
        box2[it] = lse([in1[it, k] for k in range(8)])
        for k in FAR_ORDER:
            go(box2.at[it], in2.at[it, plane], s2.at[it], r2.at[it], far[k])
        in2[it, plane] = box2[it]
        if it == 0:
            go(row_snd.at[2, 0:128], relay.at[0], sm.at[0], rm.at[0], up)
            go(row_snd.at[2, 128:256], relay.at[1], sm.at[0], rm.at[1], dn)
            row_snd[1] = permuted((y + 3) % 4)
            row_piece(0)
            row_snd[3] = permuted(y)
            kept = pltpu.make_async_copy(row_snd.at[3], row_cost.at[:, here], hbm_sem.at[4])
            kept.start()
        if it == 1:
            recv(relay.at[0], rm.at[0])
            go(relay.at[0], row_cost.at[0:128, col_of((y + 3) % 4)], sm.at[0], rm.at[2], up)
            recv(relay.at[1], rm.at[1])
            go(relay.at[1], row_cost.at[128:256, col_of((y + 1) % 4)], sm.at[0], rm.at[2], dn)
            row_piece(1)
        if it == ITERS - 1:
            recv(u_buf.at[0:3], ru.at[0])
            row_piece(2)
            recv(row_cost.at[:, col_of(yc)], rm.at[2])
            kept.wait()
            u_out[...] = jnp.concatenate([u_buf[k, 0:2, :] for k in range(4)], axis=0)
            u_copy = pltpu.make_async_copy(u_out, u_ref, hbm_sem.at[0])
            u_copy.start()
            sent(reps_v.at[0, c, 0:96], f_send.at[0])
            sent(reps_v.at[0:3, c], s_send.at[0])
            for t in range(4):
                sent(reps_v.at[t, c], c_send.at[t])
            sent(snd1, r1_send.at[0])
            sent(snd2, r2_send.at[0])
            sent(sq_buf.at[0:3], q_send.at[0])
        recv(in2.at[it, 0:15], r2.at[it])
        sent(in1.at[it, 0:7], s1.at[it])
        sent(in2.at[it, 0:15], s2.at[it])
        v = -math.log(COUNT_R) - lse([in2[it, k] for k in range(16)])

    flat = jnp.concatenate([v[g:g + 1, :] for g in range(8)], axis=1)
    pieces = split3(flat)
    row = lax.broadcasted_iota(jnp.int32, (8, 1024), 0)
    three = jnp.where(row == 0, pieces[0].astype(F32),
                      jnp.where(row == 1, pieces[1].astype(F32),
                                jnp.where(row == 2, pieces[2].astype(F32), 0.0))).astype(BF)
    got = lax.dot_general(three, rows_of(y), NT, preferred_element_type=F32)
    v_out[...] = got[0:1, :] + got[1:2, :] + got[2:3, :]
    v_copy = pltpu.make_async_copy(v_out, v_ref, hbm_sem.at[1])
    v_copy.start()
    recv(row_cost.at[:, 0:512], rm.at[3])
    sent(row_snd, sm.at[0])
    sent(u_buf.at[0:3], su.at[0])
    u_copy.wait()
    v_copy.wait()


VM = pl.BlockSpec(memory_space=pltpu.VMEM)
ANY = pl.BlockSpec(memory_space=pl.ANY)


def emit(u_ref, v_ref, cost_ref, u_out, v_out, mem_out, u_buf, v_buf, m_buf, sem):
    u_buf[...] = u_ref[...] * EPS
    v_buf[...] = v_ref[...] * EPS
    copies = [pltpu.make_async_copy(u_buf, u_out, sem.at[0]),
              pltpu.make_async_copy(v_buf, v_out, sem.at[1])]
    for cp in copies:
        cp.start()
    for h in range(2):
        half = slice(128 * h, 128 * h + 128)
        v_col = column(v_ref[:, half])
        for k in range(8):
            cols = slice(128 * k, 128 * k + 128)
            m_buf[half, cols] = (
                COUNT_S * jnp.exp((u_ref[k:k + 1, :] + v_col) - cost_ref[half, cols])).astype(BF)
        cp = pltpu.make_async_copy(m_buf.at[half], mem_out.at[half], sem.at[2 + h])
        cp.start()
        copies.append(cp)
    for cp in copies:
        cp.wait()


def on_device(scenarios, rep_index):
    dma = pltpu.SemaphoreType.DMA
    shapes = (jax.ShapeDtypeStruct((8, 128), F32),
              jax.ShapeDtypeStruct((1, 256), F32),
              jax.ShapeDtypeStruct((256, 1024), BF))
    results = pl.pallas_call(
        kernel,
        out_shape=shapes[:2] + (jax.ShapeDtypeStruct((256, 1024), F32),),
        in_specs=[pl.BlockSpec(memory_space=pltpu.HBM)] * 2,
        out_specs=(ANY, ANY, ANY),
        scratch_shapes=[
            pltpu.VMEM((ROWS, FY), BF),
            pltpu.VMEM((4, 2, 128, EXT), BF),
            pltpu.VMEM((4, 2, 4, 256, 128), F32),
            pltpu.VMEM((4, 2, 2, 176, 128), jnp.int32),
            pltpu.VMEM((4, 2, 2, 176, 128), jnp.int32),
            pltpu.VMEM((4, 2, 176, 128), jnp.int32),
            pltpu.VMEM((4, 2, 176, 128), jnp.int32),
            pltpu.VMEM((8, 8, 128), F32),
            pltpu.VMEM((8, 256, 128), F32),
            pltpu.VMEM((1, 1024), jnp.int32),
            pltpu.VMEM((1024, 1024), BF),
            pltpu.VMEM((4, 9, 8, 128), F32),
            pltpu.VMEM((5, 8, 128), F32),
            pltpu.VMEM((3, 8, 8, 128), F32),
            pltpu.VMEM((3, 16, 8, 128), F32),
            pltpu.VMEM((3, 8, 128), F32),
            pltpu.VMEM((3, 8, 128), F32),
            pltpu.VMEM((3, 2, 256, 128), F32),
            pltpu.VMEM((3, 256, 1024), BF),
            pltpu.VMEM((4, 256, 256), F32),
            pltpu.VMEM((2, 128, 256), F32),
            pltpu.VMEM((8, 128), F32),
            pltpu.VMEM((1, 256), F32),
            dma((5,)), dma((1,)), dma((7,)), dma((1,)), dma((3, 4)), dma((4,)), dma((4,)),
            dma((1,)), dma((4, 2)), dma((1,)), dma((4,)), dma((1,)), dma((1,)),
            dma((3,)), dma((3,)), dma((3,)), dma((3,)), dma((1,)), dma((1,)),
            dma((1,)), dma((4,)),
        ],
        compiler_params=pltpu.CompilerParams(
            collective_id=0, has_side_effects=True, vmem_limit_bytes=50 << 20),
        name="transport",
    )(pltpu.with_memory_space_constraint(rep_index.reshape(1, 1024), pltpu.HBM), scenarios)
    u, v, member = pl.pallas_call(
        emit,
        out_shape=shapes,
        in_specs=[VM] * 3,
        out_specs=(ANY, ANY, ANY),
        scratch_shapes=[pltpu.VMEM((8, 128), F32), pltpu.VMEM((1, 256), F32),
                        pltpu.VMEM((256, 1024), BF), dma((4,))],
        compiler_params=pltpu.CompilerParams(vmem_limit_bytes=4 << 20),
        name="emit",
    )(*results)
    return u.reshape(1024), v.reshape(256), member


def solution(mesh):
    return jax.shard_map(
        on_device,
        mesh=mesh,
        in_specs=(P("scen", "rep"), P()),
        out_specs=(P("scen"), P("rep"), P("rep", "scen")),
        check_vma=False,
    )
```
